128 devices in a mesh: ctx: 16 (over x, y_lo, core), kv: 4 (over z), rep: 2 (over y_hi).
Axes of the slice: x: 4, y: 4 (y_hi: 2, y_lo: 2; y = y_hi * 2 + y_lo), z: 4, core: 2. Of those that a mesh axis runs over, the one named last changes fastest.
Arguments:
- queries: bfloat16 [8192, 8, 12, 128], P(('rep', 'ctx'), 'kv'), parts along dimension 0, may hold values from -100 to 100
- keys: bfloat16 [8192, 8, 128], P(('rep', 'ctx'), 'kv'), parts along dimension 0, may hold values from -4 to 4
- values: bfloat16 [8192, 8, 128], P(('rep', 'ctx'), 'kv'), parts along dimension 0, may hold values from -6 to 6
- output_gradient: bfloat16 [8192, 8, 12, 128], P(('rep', 'ctx'), 'kv'), parts along dimension 0, may hold values from -60 to 60
- band_start: int32 [8192], P(('rep', 'ctx')), parts along dimension 0, may hold values from 0 to 4095, as said below
Outputs:
- grad_query: float32 [8192, 8, 12, 128], P(('rep', 'ctx'), 'kv'), parts along dimension 0
- grad_key: float32 [8192, 8, 128], P(('rep', 'ctx'), 'kv'), parts along dimension 0
- grad_value: float32 [8192, 8, 128], P(('rep', 'ctx'), 'kv'), parts along dimension 0
The draws below stay inside these ranges and needn't reach their ends.
There are 2 independent parts, one for each index of `rep`. The reference program is written for one: setup_inputs(seed, part) draws one part's arguments, and reference() takes and returns one part's arrays. A program takes and returns all parts, laid end to end along the dimension named above; each array names one. Nothing has to cross between parts.
Inputs may be any that keep to these rules, and one draw needn't show every extreme that they name: For every row i, i - 2047 <= band_start[i] <= i and band_start[i] >= 0; the lower end i - 2047 is reached at some rows wherever i >= 2047.
All inputs are finite; a program needn't handle non-finite values.
Results may differ from the reference program's by a relative error of at most 0.003.
Values may be sent and summed in bfloat16 or wider, within the bound.
A program may use at most 256 MiB of HBM per device.

```python
import jax
import jax.numpy as jnp
from jax import lax

KEY_VALUE_HEADS = 8
QUERY_PER_KEY = 12
HEAD_WIDTH = 128
TOK_DEV = 256
WINDOW = 2048
SEQUENCE_TOKENS = 4096


def paired_draw(key):
    base = jax.random.fold_in(key, 11)
    leading_key, following_key = jax.random.split(base, 2)
    sampled_keys = jnp.clip(jax.random.normal(following_key, (SEQUENCE_TOKENS, KEY_VALUE_HEADS, HEAD_WIDTH), jnp.float32), -4.0, 4.0)
    sampled_queries = jnp.clip(jax.random.normal(leading_key, (SEQUENCE_TOKENS, KEY_VALUE_HEADS, QUERY_PER_KEY, HEAD_WIDTH), jnp.float32), -4.0, 4.0)
    return (sampled_queries, sampled_keys)


def draw_queries(key, part):
    return paired_draw(key)[0].astype(jnp.bfloat16)


def draw_keys(key, part):
    return paired_draw(key)[1].astype(jnp.bfloat16)


def draw_band_start(key, part):
    base = jax.random.fold_in(key, 23)
    position = jnp.arange(SEQUENCE_TOKENS, dtype=jnp.int32)
    span_length = jax.random.randint(base, (SEQUENCE_TOKENS,), 1, WINDOW + 1)
    span_length = jnp.where(position % TOK_DEV == TOK_DEV - 1, WINDOW, span_length)
    return jnp.maximum(0, position - span_length + 1).astype(jnp.int32)


def levels(own_key, shape, pieces, low, high):
    loudness, own = 1.0, jax.random.fold_in(own_key, 6)
    for dim, shards_of in pieces:
        draws = jnp.exp(jax.random.uniform(jax.random.fold_in(own, dim), (shards_of,), jnp.float32, low / len(pieces), high / len(pieces)))
        loudness = loudness * jnp.repeat(draws, shape[dim] // shards_of).reshape([-1 if axis == dim else 1 for axis in range(len(shape))])
    return loudness


def bell_draw(own_key, dims, spread, most, pieces=(), kind=jnp.bfloat16):
    entries = jax.random.normal(own_key, dims, jnp.float32) * spread
    if len(pieces) > 0:
        entries = levels(own_key, dims, pieces, -0.22, 0.18) * entries
    return jnp.clip(entries, min=-most, max=most).astype(kind)


def setup_inputs(seed: int = 0, part: int = 0) -> dict:
    streams_of = jax.random.split(jax.random.key(seed), 6)
    part_splits = jax.random.split(jax.random.fold_in(streams_of[5], part), 6)
    queries = draw_queries(jax.random.fold_in(jax.random.fold_in(streams_of[5], part), 71), part)
    keys = draw_keys(jax.random.fold_in(jax.random.fold_in(streams_of[5], part), 71), part)
    values = bell_draw(part_splits[2], (SEQUENCE_TOKENS, KEY_VALUE_HEADS, HEAD_WIDTH), 1.0, 6.0, ((0, 16), (1, 4)))
    output_gradient = bell_draw(part_splits[3], (SEQUENCE_TOKENS, KEY_VALUE_HEADS, QUERY_PER_KEY, HEAD_WIDTH), 10.0, 60.0, ((0, 16), (1, 4)))
    band_start = draw_band_start(jax.random.fold_in(jax.random.fold_in(streams_of[5], part), 71), part)
    return dict(queries=queries, keys=keys, values=values, output_gradient=output_gradient, band_start=band_start)


def head_grads(query_head, key_head, value_head, cotangent_head, band_start):
    seq_len = query_head.shape[0]
    head_size = query_head.shape[2]
    scaling = head_size ** -0.5
    key_span = WINDOW + TOK_DEV
    padding = jnp.zeros((WINDOW, head_size), key_head.dtype)
    key_padded = jnp.concatenate([padding, key_head], 0)
    value_padded = jnp.concatenate([padding, value_head], 0)
    block_count = seq_len // TOK_DEV

    def one_block(carried, block_index):
        key_sum, value_sum = carried
        first_row = (block_index * TOK_DEV).astype(jnp.int32)
        query_block = lax.dynamic_slice_in_dim(query_head, first_row, TOK_DEV, 0).astype(jnp.float32)
        cotangent_block = lax.dynamic_slice_in_dim(cotangent_head, first_row, TOK_DEV, 0).astype(jnp.float32)
        key_block = lax.dynamic_slice_in_dim(key_padded, first_row, key_span, 0).astype(jnp.float32)
        value_block = lax.dynamic_slice_in_dim(value_padded, first_row, key_span, 0).astype(jnp.float32)
        start_block = lax.dynamic_slice_in_dim(band_start, first_row, TOK_DEV, 0)
        row_pos = first_row + jnp.arange(TOK_DEV, dtype=jnp.int32)
        key_pos = first_row - WINDOW + jnp.arange(key_span, dtype=jnp.int32)
        allowed = (key_pos[None, :] >= start_block[:, None]) & (key_pos[None, :] <= row_pos[:, None])
        allowed = allowed[:, None, :]
        scores = jnp.einsum('rgd,kd->rgk', query_block, key_block) * scaling
        grad_probs = jnp.einsum('rgd,kd->rgk', cotangent_block, value_block)
        row_max = jnp.max(jnp.where(allowed, scores, -1e30), -1)
        log_total = row_max + jnp.log(jnp.sum(jnp.where(allowed, jnp.exp(scores - row_max[..., None]), 0.0), -1))
        weights = jnp.where(allowed, jnp.exp(scores - log_total[..., None]), 0.0)
        dot_sum = jnp.sum(weights * grad_probs, -1)
        weights_bf = lax.optimization_barrier(weights.astype(jnp.bfloat16)).astype(jnp.float32)
        grad_scores = lax.optimization_barrier((weights * (grad_probs - dot_sum[..., None])).astype(jnp.bfloat16)).astype(jnp.float32)
        query_grad = jnp.einsum('rgk,kd->rgd', grad_scores, key_block) * scaling
        key_part = jnp.einsum('rgk,rgd->kd', grad_scores, query_block) * scaling
        value_part = jnp.einsum('rgk,rgd->kd', weights_bf, cotangent_block)
        old_keys = lax.dynamic_slice_in_dim(key_sum, first_row, key_span, 0)
        key_sum = lax.dynamic_update_slice_in_dim(key_sum, old_keys + key_part, first_row, 0)
        old_values = lax.dynamic_slice_in_dim(value_sum, first_row, key_span, 0)
        value_sum = lax.dynamic_update_slice_in_dim(value_sum, old_values + value_part, first_row, 0)
        return (key_sum, value_sum), query_grad

    zeros_init = jnp.zeros((seq_len + WINDOW, head_size), jnp.float32)
    (key_sum, value_sum), query_grads = lax.scan(one_block, (zeros_init, zeros_init), jnp.arange(block_count, dtype=jnp.int32))
    query_grads = query_grads.reshape(seq_len, query_head.shape[1], head_size)
    return query_grads, key_sum[WINDOW:], value_sum[WINDOW:]


def reference(queries, keys, values, output_gradient, band_start):
    def per_head(packed):
        return head_grads(packed[0], packed[1], packed[2], packed[3], band_start)

    stacked = (jnp.transpose(queries, (1, 0, 2, 3)), jnp.transpose(keys, (1, 0, 2)),
               jnp.transpose(values, (1, 0, 2)), jnp.transpose(output_gradient, (1, 0, 2, 3)))
    query_grads, key_grads, value_grads = lax.map(per_head, stacked)
    return (jnp.transpose(query_grads, (1, 0, 2, 3)), jnp.transpose(key_grads, (1, 0, 2)),
            jnp.transpose(value_grads, (1, 0, 2)))
```

```python
import functools, math
import jax, jax.numpy as jnp
from jax import lax
from jax.experimental import pallas as pl
from jax.experimental.pallas import tpu as pltpu
from jax.sharding import PartitionSpec as P

R=256; G=12; H=2; D=128; W=WINDOW=2048; CH=128
KW=W+128
NC=KW//CH
SC=D**-0.5
C2=SC*math.log2(math.e)
NEG=-1e30
NT=(((1,),(1,)),((),()))
NN=(((1,),(0,)),((),()))
TN=(((0,),(0,)),((),()))
def dot(a,b,dims): return lax.dot_general(a,b,dims,preferred_element_type=jnp.float32)

def prologue(q2,do2,bs,base,qs,dos,tmp,bias):
    for src,dst in ((q2,qs),(do2,dos)):
        tmp[...]=src[...].astype(jnp.float32)
        def body(g,_):
            for h in range(H):
                dst[h,g]=tmp[pl.ds(g*2+h,R,stride=24),:].astype(jnp.bfloat16)
            return 0
        lax.fori_loop(0,G,body,0)
    row=base+lax.broadcasted_iota(jnp.int32,(1,R),1)
    st=bs[...]
    for half in range(2):
        sl=slice(half*128,half*128+128)
        def body(c,_):
            key=base-W+half*128+c*CH+lax.broadcasted_iota(jnp.int32,(CH,128),0)
            ok=(key>=st[:,sl])&(key<=row[:,sl])
            bias[half,pl.ds(pl.multiple_of(c*CH,CH),CH),:]=jnp.where(ok,0.0,NEG)
            return 0
        lax.fori_loop(0,NC,body,0)

def stageA(h,gp,half,qs,dos,kv,bias,p,dp,st):
    qu=qs[h,pl.ds(gp*2,2),half*128:half*128+128,:].reshape(256,D)
    du=dos[h,pl.ds(gp*2,2),half*128:half*128+128,:].reshape(256,D)
    m=jnp.full((1,8,256),NEG,jnp.float32)
    l=jnp.zeros((1,8,256),jnp.float32); dd=l
    for c in range(NC):
        k0=half*128+c*CH
        s=dot(kv[h,0,k0:k0+CH,:],qu,NT)*C2
        g=dot(kv[h,1,k0:k0+CH,:],du,NT)
        b=bias[half,c*CH:(c+1)*CH,:]
        s=(s+jnp.concatenate([b,b],1)).reshape(CH//8,8,256)
        g=g.reshape(CH//8,8,256)
        mn=jnp.maximum(m,jnp.max(s,0,keepdims=True))
        al=jnp.exp2(m-mn)
        e=jnp.exp2(s-mn)
        l=l*al+jnp.sum(e,0,keepdims=True)
        dd=dd*al+jnp.sum(e*g,0,keepdims=True)
        p[c]=e; dp[c]=g
        st[c]=mn[0]
        m=mn
    mm=jnp.max(m,1,keepdims=True)
    e=jnp.exp2(m-mm)
    lt=jnp.sum(l*e,1,keepdims=True)
    il=1.0/lt
    ds=jnp.sum(dd*e,1,keepdims=True)*il
    for c in range(NC):
        st[c]=jnp.exp2(st[c]-mm[0])*il[0]
    st[NC]=jnp.broadcast_to(ds[0],(8,256))

def stageB(h,gp,half,qs,dos,kv,p,dp,st,dkv,dq):
    qu=qs[h,pl.ds(gp*2,2),half*128:half*128+128,:].reshape(256,D)
    du=dos[h,pl.ds(gp*2,2),half*128:half*128+128,:].reshape(256,D)
    dsum=st[NC][None]
    acc=jnp.zeros((D,256),jnp.float32)
    for c in range(NC):
        k0=half*128+c*CH
        w=p[c]*st[c][None]
        x=w*(dp[c]-dsum)
        wb=w.reshape(CH,256).astype(jnp.bfloat16)
        xb=x.reshape(CH,256).astype(jnp.bfloat16)
        dkv[h,1,k0:k0+CH,:]+=dot(wb,du,NN)
        dkv[h,0,k0:k0+CH,:]+=dot(xb,qu,NN)
        acc=acc+dot(kv[h,0,k0:k0+CH,:],xb,TN)
    acc=acc.T*SC
    for i in range(2):
        dq[pl.ds(half*128*24+(gp*2+i)*2+h,128,stride=24),:]=acc[i*128:(i+1)*128]

def kernel(base_ref,q2,do2,kv,bs,dq,dkv,qs,dos,tmp,bias,p0,dp0,st0,p1,dp1,st1):
    base=base_ref[0]
    prologue(q2,do2,bs,base,qs,dos,tmp,bias)
    dkv[...]=jnp.zeros_like(dkv)
    stageA(0,0,0,qs,dos,kv,bias,p0,dp0,st0)
    def body(it,_):
        h=it//6; gp=it%6
        nx=jnp.minimum(it+1,11); h2=nx//6; gp2=nx%6
        stageA(h,gp,1,qs,dos,kv,bias,p1,dp1,st1)
        stageB(h,gp,0,qs,dos,kv,p0,dp0,st0,dkv,dq)
        stageA(h2,gp2,0,qs,dos,kv,bias,p0,dp0,st0)
        stageB(h,gp,1,qs,dos,kv,p1,dp1,st1,dkv,dq)
        return 0
    lax.fori_loop(0,12,body,0)

def call(base,q2,do2,kv,bs,kernel=kernel,extra=()):
    vm=pl.BlockSpec(memory_space=pltpu.VMEM)
    return pl.pallas_call(kernel,
        out_shape=(jax.ShapeDtypeStruct((R*24,D),jnp.float32),jax.ShapeDtypeStruct((H,2,W+R,D),jnp.float32)),
        in_specs=[pl.BlockSpec(memory_space=pltpu.SMEM),vm,vm,vm,vm],out_specs=(vm,vm),
        scratch_shapes=[pltpu.VMEM((H,G,R,D),jnp.bfloat16)]*2+[pltpu.VMEM((R*24,D),jnp.float32),pltpu.VMEM((2,KW,128),jnp.float32)]
          +[pltpu.VMEM((NC,CH//8,8,256),jnp.float32),pltpu.VMEM((NC,CH//8,8,256),jnp.float32),pltpu.VMEM((NC+1,8,256),jnp.float32)]*2+list(extra),
        compiler_params=pltpu.CompilerParams(vmem_limit_bytes=62*2**20),
    )(base,q2,do2,kv,bs)


def passed_along(block, distance):
    devices = range(lax.axis_size("ctx"))
    route = [(i - distance, i) for i in devices if i - distance in devices]
    return lax.ppermute(block, "ctx", route)


def shards(queries, keys, values, output_gradient, band_start):
    base=(lax.axis_index("ctx")*R).astype(jnp.int32).reshape(1)
    q2=queries.transpose(0,2,1,3).reshape(R*24,D)
    d2=output_gradient.transpose(0,2,1,3).reshape(R*24,D)
    own=jnp.stack([keys.transpose(1,0,2),values.transpose(1,0,2)],1)
    reach=W//R
    kv=jnp.concatenate([passed_along(own,o) for o in range(reach,0,-1)]+[own],2)
    dq,dkv=call(base,q2,d2,kv,band_start.reshape(1,R))
    total=dkv[:,:,W:]
    for o in range(1,reach+1):
        part=dkv[:,:,W-o*R:W-o*R+R].astype(jnp.bfloat16)
        total=total+passed_along(part,-o).astype(jnp.float32)
    total=total.transpose(1,2,0,3)
    return dq.reshape(R,G,H,D).transpose(0,2,1,3),total[0]*SC,total[1]


def solution(mesh):
    rows = P(("rep", "ctx"), "kv", None, None)
    keyed = P(("rep", "ctx"), "kv", None)
    return jax.shard_map(shards, mesh=mesh, in_specs=(rows, keyed, keyed, rows, P(("rep", "ctx"))),
        out_specs=(rows, keyed, keyed), check_vma=False)
```

```python
import functools, math
import jax, jax.numpy as jnp
from jax import lax
from jax.experimental import pallas as pl
from jax.experimental.pallas import tpu as pltpu
from jax.sharding import PartitionSpec as P

R = 256
G = 12
H = 2
D = 128
W = 2048
CH = 128
KW = W + 128
NC = KW // CH
NB = W // R
SC = D**-0.5
C2 = SC * math.log2(math.e)
NEG = -1e30
NT = (((1,), (1,)), ((), ()))
NN = (((1,), (0,)), ((), ()))
TN = (((0,), (0,)), ((), ()))
MESH = pl.DeviceIdType.MESH
BF = jnp.bfloat16
F32 = jnp.float32


def dot(a, b, dims):
    return lax.dot_general(a, b, dims, preferred_element_type=F32)


def keys_of(kv, h, kind, k0):
    return kv[h, kind, k0 // R, k0 % R : k0 % R + CH, :]


def stage_a(h, gp, half, qs, dos, kv, bias, p, dp, st):
    rows = slice(half * 128, half * 128 + 128)
    qu = qs[h, pl.ds(gp * 2, 2), rows, :].reshape(256, D)
    du = dos[h, pl.ds(gp * 2, 2), rows, :].reshape(256, D)
    m = jnp.full((1, 8, 256), NEG, F32)
    l = jnp.zeros((1, 8, 256), F32)
    dd = l
    for c in range(NC):
        k0 = half * 128 + c * CH
        s = dot(keys_of(kv, h, 0, k0), qu, NT) * C2
        g = dot(keys_of(kv, h, 1, k0), du, NT)
        b = bias[half, c * CH : (c + 1) * CH, :]
        s = (s + jnp.concatenate([b, b], 1)).reshape(CH // 8, 8, 256)
        g = g.reshape(CH // 8, 8, 256)
        mn = jnp.maximum(m, jnp.max(s, 0, keepdims=True))
        al = jnp.exp2(m - mn)
        e = jnp.exp2(s - mn)
        l = l * al + jnp.sum(e, 0, keepdims=True)
        dd = dd * al + jnp.sum(e * g, 0, keepdims=True)
        p[c] = e
        dp[c] = g
        st[c] = mn[0]
        m = mn
    mm = jnp.max(m, 1, keepdims=True)
    e = jnp.exp2(m - mm)
    il = 1.0 / jnp.sum(l * e, 1, keepdims=True)
    ds = jnp.sum(dd * e, 1, keepdims=True) * il
    for c in range(NC):
        st[c] = jnp.exp2(st[c] - mm[0]) * il[0]
    st[NC] = jnp.broadcast_to(ds[0], (8, 256))


def stage_b(h, gp, half, qs, dos, kv, p, dp, st, dkv, dq):
    rows = slice(half * 128, half * 128 + 128)
    qu = qs[h, pl.ds(gp * 2, 2), rows, :].reshape(256, D)
    du = dos[h, pl.ds(gp * 2, 2), rows, :].reshape(256, D)
    dsum = st[NC][None]
    acc = jnp.zeros((D, 256), F32)
    for c in range(NC):
        k0 = half * 128 + c * CH
        w = p[c] * st[c][None]
        x = w * (dp[c] - dsum)
        wb = w.reshape(CH, 256).astype(BF)
        xb = x.reshape(CH, 256).astype(BF)
        s, o = k0 // R, k0 % R
        dkv[h, 1, s, o : o + CH, :] += dot(wb, du, NN)
        dkv[h, 0, s, o : o + CH, :] += dot(xb, qu, NN)
        acc = acc + dot(keys_of(kv, h, 0, k0), xb, TN)
    acc = acc.T * SC
    for i in range(2):
        dq[pl.ds(half * 128 * 24 + (gp * 2 + i) * 2 + h, 128, stride=24), :] = acc[i * 128 : (i + 1) * 128]


def kernel(q2, do2, own, bs, dq, gkv, qv, dov, qs, dos, tmp, bias, kv, dkv, p0, dp0, st0, p1, dp1, st1,
           cs, cr, ys, yr, xs, xr, lsem, gs, gr, css, crs, yss, yrs, xss, xrs):
    me = lax.axis_index("ctx")
    x = me // 4
    yl = (me // 2) % 2
    c = me % 2
    base = me * R
    core = me + 1 - 2 * c
    ypar = me + 2 - 4 * yl

    loads = [pltpu.make_async_copy(q2, qv, lsem.at[0]), pltpu.make_async_copy(do2, dov, lsem.at[1])]
    for a in loads:
        a.start()

    barrier = pltpu.get_barrier_semaphore()
    for t in (core, ypar):
        pl.semaphore_signal(barrier, inc=1, device_id={"ctx": t}, device_id_type=MESH)

    @pl.when(x < 3)
    def _():
        pl.semaphore_signal(barrier, inc=1, device_id={"ctx": me + 4}, device_id_type=MESH)

    @pl.when(x > 0)
    def _():
        pl.semaphore_signal(barrier, inc=1, device_id={"ctx": me - 4}, device_id_type=MESH)

    pl.semaphore_wait(barrier, 2 + jnp.where(x < 3, 1, 0) + jnp.where(x > 0, 1, 0))

    def rc(src, dst, ss, rs, to):
        return pltpu.make_async_remote_copy(src_ref=src, dst_ref=dst, send_sem=ss, recv_sem=rs,
                                            device_id={"ctx": to}, device_id_type=MESH)

    def routes(h, kind):
        def one(num, src_slot, slot, to):
            src = own.at[h, kind] if src_slot == 8 else kv.at[h, kind, src_slot]
            return rc(src, kv.at[h, kind, slot], gs.at[h, kind, num], gr.at[h, kind, slot], to)

        return {
            0: (x < 3, lambda: one(0, 8, 4, me + 4)),
            1: (yl == 0, lambda: one(1, 8, 6, ypar)),
            2: (c == 0, lambda: one(2, 8, 7, core)),
            3: ((x > 0) & (x < 3), lambda: one(3, 4, 0, me + 4)),
            4: (x > 0, lambda: one(4, 4, 2 + 4 * yl, ypar)),
            5: (x > 0, lambda: one(5, 4, 3 + 2 * c, core)),
            6: (me >= 2, lambda: one(6, 6, 5 + 2 * c, core)),
            7: ((x > 1) & (yl == 1), lambda: one(7, 0, 2, ypar)),
            8: ((x > 1) & (c == 1), lambda: one(8, 0, 1, core)),
            9: (me >= 6, lambda: one(9, 2, 1 + 2 * c, core)),
        }

    def go(h, nums):
        for kind in range(2):
            r = routes(h, kind)
            for n in nums:
                pl.when(r[n][0])(lambda n=n, r=r: r[n][1]().start())

    def arrived(h, kind, slot):
        @pl.when(me >= 8 - slot)
        def _():
            rc(kv.at[h, kind, slot], kv.at[h, kind, slot], gs.at[h, kind, 0], gr.at[h, kind, slot], core).wait_recv()

    def after(h, slot, nums):
        for kind in range(2):
            arrived(h, kind, slot)
            r = routes(h, kind)
            for n in nums:
                pl.when(r[n][0])(lambda n=n, r=r: r[n][1]().start())

    def odd_slots(h):
        for kind in range(2):
            for slot in (7, 5, 3, 1):
                arrived(h, kind, slot)

    def core_copy(h, kind, j):
        return rc(cs.at[h, kind, j], cr.at[h, kind, j], css.at[h, kind, j], crs.at[h, kind, j], core)

    def y_copy(h, kind, j):
        return rc(ys.at[h, kind, j], yr.at[h, kind, j], yss.at[h, kind, j], yrs.at[h, kind, j], ypar)

    def x_copy(h, kind, j):
        return rc(xs.at[h, kind, j], xr.at[h, kind, j], xss.at[h, kind, j], xrs.at[h, kind, j], me - 4)

    def core_send(h):
        for j in (3, 0, 1, 2):
            @pl.when(me >= 2 * j + 1)
            def _():
                for kind in (1, 0):
                    cs[h, kind, j] = dkv[h, kind, 7 - 2 * j].astype(BF)
                    core_copy(h, kind, j).start()

    def core_add(h, kind, j):
        @pl.when(core >= 2 * j + 1)
        def _():
            core_copy(h, kind, j).wait_recv()
            to = 8 - 2 * j - 2 * c
            dkv[h, kind, to] += cr[h, kind, j].astype(F32)

    def y_send(h, kind, j):
        @pl.when(me >= 2 + 4 * j)
        def _():
            ys[h, kind, j] = dkv[h, kind, 6 - 4 * j].astype(BF)
            y_copy(h, kind, j).start()

    def y_add(h, kind, j):
        @pl.when(ypar >= 2 + 4 * j)
        def _():
            y_copy(h, kind, j).wait_recv()
            to = 8 - 4 * (j + yl)
            dkv[h, kind, to] += yr[h, kind, j].astype(F32)

    def x_send(h, kind, j):
        @pl.when(x >= 2 - j)
        def _():
            xs[h, kind, j] = dkv[h, kind, 4 * j].astype(BF)
            x_copy(h, kind, j).start()

    def x_add(h, kind, j):
        @pl.when((x < 3) & (x >= 1 - j))
        def _():
            x_copy(h, kind, j).wait_recv()
            dkv[h, kind, 4 + 4 * j] += xr[h, kind, j].astype(F32)

    def red1(h):
        for kind in (1, 0):
            for j in (3, 2):
                core_add(h, kind, j)
            y_send(h, kind, 1)
        for kind in (1, 0):
            for j in (0, 1):
                core_add(h, kind, j)
            y_send(h, kind, 0)

    def red2(h):
        for kind in (1, 0):
            y_add(h, kind, 1)
            x_send(h, kind, 0)

    def red3(h):
        for kind in (1, 0):
            y_add(h, kind, 0)
        for kind in (1, 0):
            x_add(h, kind, 0)
            x_send(h, kind, 1)

    def red4(h):
        for kind in (1, 0):
            x_add(h, kind, 1)
            t = dkv[h, kind, 8]
            gkv[kind, pl.ds(h, R, stride=2), :] = t * SC if kind == 0 else t

    go(0, (0, 1, 2))

    for h in range(H):
        for kind in range(2):
            kv[h, kind, 8] = own[h, kind]
    for slot in range(8):
        @pl.when(me < 8 - slot)
        def _():
            for h in range(H):
                for kind in range(2):
                    kv[h, kind, slot] = jnp.zeros((R, D), BF)
    row = base + lax.broadcasted_iota(jnp.int32, (1, R), 1)
    first = bs[...]
    for half in range(2):
        sl = slice(half * 128, half * 128 + 128)

        def body(i, _):
            key = base - W + half * 128 + i * CH + lax.broadcasted_iota(jnp.int32, (CH, 128), 0)
            ok = (key >= first[:, sl]) & (key <= row[:, sl])
            bias[half, pl.ds(pl.multiple_of(i * CH, CH), CH), :] = jnp.where(ok, 0.0, NEG)
            return 0

        lax.fori_loop(0, NC, body, 0)

    def unpack(src, dst):
        tmp[...] = src[...].astype(F32)

        def body(g, _):
            for h in range(H):
                dst[h, g] = tmp[pl.ds(g * 2 + h, R, stride=24), :].astype(BF)
            return 0

        lax.fori_loop(0, G, body, 0)

    loads[0].wait()
    unpack(qv, qs)
    after(0, 4, (3, 4, 5))
    loads[1].wait()
    unpack(dov, dos)
    dkv[...] = jnp.zeros_like(dkv)
    after(0, 6, (6,))
    after(0, 0, (7, 8))
    after(0, 2, (9,))
    odd_slots(0)

    stage_a(0, 0, 0, qs, dos, kv, bias, p0, dp0, st0)

    steps = {
        0: lambda: go(1, (0, 1, 2)),
        1: lambda: after(1, 4, (3, 4, 5)),
        2: lambda: after(1, 6, (6,)),
        3: lambda: after(1, 0, (7, 8)),
        4: lambda: after(1, 2, (9,)),
        5: lambda: odd_slots(1),
        6: lambda: core_send(0),
        7: lambda: red1(0),
        9: lambda: red2(0),
        10: lambda: red3(0),
        11: lambda: red4(0),
    }

    def unit(it, _):
        for k, f in steps.items():
            pl.when(it == k)(f)
        h = it // 6
        gp = it % 6
        nx = jnp.minimum(it + 1, 11)
        stage_a(h, gp, 1, qs, dos, kv, bias, p1, dp1, st1)
        stage_b(h, gp, 0, qs, dos, kv, p0, dp0, st0, dkv, dq)
        stage_a(nx // 6, nx % 6, 0, qs, dos, kv, bias, p0, dp0, st0)
        stage_b(h, gp, 1, qs, dos, kv, p1, dp1, st1, dkv, dq)
        return 0

    lax.fori_loop(0, 12, unit, 0)
    core_send(1)
    red1(1)
    red2(1)
    red3(1)
    red4(1)
    for h in range(H):
        for kind in range(2):
            r = routes(h, kind)
            for n in range(10):
                pl.when(r[n][0])(lambda n=n, r=r: r[n][1]().wait_send())
            for j in range(4):
                pl.when(me >= 2 * j + 1)(lambda h=h, kind=kind, j=j: core_copy(h, kind, j).wait_send())
            for j in range(2):
                pl.when(me >= 2 + 4 * j)(lambda h=h, kind=kind, j=j: y_copy(h, kind, j).wait_send())
                pl.when(x >= 2 - j)(lambda h=h, kind=kind, j=j: x_copy(h, kind, j).wait_send())


def fused(q2, do2, own, bs):
    vm = pl.BlockSpec(memory_space=pltpu.VMEM)
    hbm = pl.BlockSpec(memory_space=pl.ANY)
    tile = pltpu.VMEM((NC, CH // 8, 8, 256), F32)
    stats = pltpu.VMEM((NC + 1, 8, 256), F32)
    dma = pltpu.SemaphoreType.DMA
    return pl.pallas_call(
        kernel,
        out_shape=(jax.ShapeDtypeStruct((R * 24, D), F32), jax.ShapeDtypeStruct((2, R * 2, D), F32)),
        in_specs=[hbm, hbm, vm, vm],
        out_specs=(vm, vm),
        scratch_shapes=[
            pltpu.VMEM((R * 24, D), BF), pltpu.VMEM((R * 24, D), BF),
            pltpu.VMEM((H, G, R, D), BF), pltpu.VMEM((H, G, R, D), BF),
            pltpu.VMEM((R * 24, D), F32), pltpu.VMEM((2, KW, 128), F32),
            pltpu.VMEM((H, 2, NB + 1, R, D), BF), pltpu.VMEM((H, 2, NB + 1, R, D), F32),
            tile, tile, stats, tile, tile, stats,
            pltpu.VMEM((H, 2, 4, R, D), BF), pltpu.VMEM((H, 2, 4, R, D), BF),
            pltpu.VMEM((H, 2, 2, R, D), BF), pltpu.VMEM((H, 2, 2, R, D), BF),
            pltpu.VMEM((H, 2, 2, R, D), BF), pltpu.VMEM((H, 2, 2, R, D), BF),
            dma((2,)), dma((H, 2, 10)), dma((H, 2, 9)),
            dma((H, 2, 4)), dma((H, 2, 4)), dma((H, 2, 2)), dma((H, 2, 2)), dma((H, 2, 2)), dma((H, 2, 2)),
        ],
        compiler_params=pltpu.CompilerParams(collective_id=0, has_side_effects=True, vmem_limit_bytes=62 * 2**20),
    )(q2, do2, own, bs)


def shards(queries, keys, values, output_gradient, band_start):
    q2 = queries.transpose(0, 2, 1, 3).reshape(R * 24, D)
    d2 = output_gradient.transpose(0, 2, 1, 3).reshape(R * 24, D)
    own = jnp.stack([keys.transpose(1, 0, 2), values.transpose(1, 0, 2)], 1)
    dq, gkv = fused(q2, d2, own, band_start.reshape(1, R))
    gkv = gkv.reshape(2, R, H, D)
    return dq.reshape(R, G, H, D).transpose(0, 2, 1, 3), gkv[0], gkv[1]


def solution(mesh):
    rows = P(("rep", "ctx"), "kv", None, None)
    keyed = P(("rep", "ctx"), "kv", None)
    return jax.shard_map(shards, mesh=mesh, in_specs=(rows, keyed, keyed, rows, P(("rep", "ctx"))),
                         out_specs=(rows, keyed, keyed), check_vma=False)
```

```python
import functools, math
import jax, jax.numpy as jnp
from jax import lax
from jax.experimental import pallas as pl
from jax.experimental.pallas import tpu as pltpu
from jax.sharding import PartitionSpec as P

R = 256
G = 12
H = 2
D = 128
W = 2048
CH = 128
SZ = 512
KW = W + 128
NC = KW // CH
NB = W // R
SC = D**-0.5
C2 = SC * math.log2(math.e)
NEG = -1e30
VLIM = 63 * 2**20
NT = (((1,), (1,)), ((), ()))
NN = (((1,), (0,)), ((), ()))
TN = (((0,), (0,)), ((), ()))
MESH = pl.DeviceIdType.MESH
BF = jnp.bfloat16
F32 = jnp.float32


def dot(a, b, dims):
    return lax.dot_general(a, b, dims, preferred_element_type=F32)


def chunks():
    return [(o, min(SZ, KW - o)) for o in range(0, KW, SZ)]


def unit_rows(ref, h, gp, half):
    return ref[h, pl.ds(gp * 2, 2), half * 128 : half * 128 + 128, :].reshape(256, D)


def stage_a(h, gp, half, qs, dos, kv, bias, p, dp, st):
    qu = unit_rows(qs, h, gp, half)
    du = unit_rows(dos, h, gp, half)
    m = jnp.full((1, 8, 256), NEG, F32)
    l = jnp.zeros((1, 8, 256), F32)
    dd = l
    for i, (o, n) in enumerate(chunks()):
        keys = slice(half * 128 + o, half * 128 + o + n)
        s = dot(kv[h, 0, keys, :], qu, NT) * C2
        g = dot(kv[h, 1, keys, :], du, NT)
        b = bias[half, o : o + n, :]
        s = (s + jnp.concatenate([b, b], 1)).reshape(n // 8, 8, 256)
        g = g.reshape(n // 8, 8, 256)
        mn = jnp.maximum(m, jnp.max(s, 0, keepdims=True))
        al = jnp.exp2(m - mn)
        e = jnp.exp2(s - mn)
        l = l * al + jnp.sum(e, 0, keepdims=True)
        dd = dd * al + jnp.sum(e * g, 0, keepdims=True)
        p[o // 8 : (o + n) // 8] = e
        dp[o // 8 : (o + n) // 8] = g
        st[i] = mn[0]
        m = mn
        yield 1
    mm = jnp.max(m, 1, keepdims=True)
    e = jnp.exp2(m - mm)
    il = 1.0 / jnp.sum(l * e, 1, keepdims=True)
    ds = jnp.sum(dd * e, 1, keepdims=True) * il
    nc = len(chunks())
    for i in range(nc):
        st[i] = jnp.exp2(st[i] - mm[0]) * il[0]
    st[nc] = jnp.broadcast_to(ds[0], (8, 256))
    yield 1


def stage_b(h, gp, half, qs, dos, p, dp, st, dkv, dss):
    qu = unit_rows(qs, h, gp, half)
    du = unit_rows(dos, h, gp, half)
    dsum = st[len(chunks())][None]
    u = (h * 6 + gp) * 2 + half
    for i, (o, n) in enumerate(chunks()):
        keys = slice(half * 128 + o, half * 128 + o + n)
        w = p[o // 8 : (o + n) // 8] * st[i][None]
        x = w * (dp[o // 8 : (o + n) // 8] - dsum)
        wb = w.reshape(n, 256).astype(BF)
        xb = x.reshape(n, 256).astype(BF)
        dkv[h, 1, keys, :] += dot(wb, du, NN)
        dkv[h, 0, keys, :] += dot(xb, qu, NN)
        dss[u, o : o + n, :] = xb
        yield 1


def query_gradients(half, first, last, kt, dss, dq):
    def body(it, _):
        h = it // 6
        gp = it % 6
        t = dot(kt[h, :, half * 128 : half * 128 + KW], dss[it * 2 + half], NN).T
        for i in range(2):
            dq[pl.ds(half * 128 * 24 + (gp * 2 + i) * 2 + h, 128, stride=24), :] = t[i * 128 : (i + 1) * 128]
        return 0

    lax.fori_loop(first, last, body, 0)


def together(*steps):
    steps = list(steps)
    while steps:
        for s in list(steps):
            if next(s, 0) == 0:
                steps.remove(s)


def kernel(q2, do2, k2, v2, bs, dq, gk, gv, dqo, dov, dss, qs, dos, tmp, bias, kv, kt, dkv, p0, dp0, st0, p1, dp1, st1,
           cs, cr, ys, yr, xs, xr, lsem, gs, gr, css, crs, yss, yrs, xss, xrs):
    me = lax.axis_index("ctx")
    x = me // 4
    yl = (me // 2) % 2
    c = me % 2
    base = me * R
    core = me + 1 - 2 * c
    ypar = me + 2 - 4 * yl

    loads = [pltpu.make_async_copy(q2, dqo, lsem.at[0]), pltpu.make_async_copy(do2, dov, lsem.at[1])]
    for a in loads:
        a.start()

    for kind, src in enumerate((k2, v2)):
        tmp[kind * 2 * R : (kind + 1) * 2 * R] = src[...].astype(F32)
        for h in range(H):
            kv[h, kind, NB * R :] = tmp[pl.ds(kind * 2 * R + h, R, stride=2), :].astype(BF)

    barrier = pltpu.get_barrier_semaphore()
    for t in (core, ypar):
        pl.semaphore_signal(barrier, inc=1, device_id={"ctx": t}, device_id_type=MESH)

    for there, t in ((x < 3, me + 4), (x > 0, me - 4), (x < 2, me + 8), (x > 1, me - 8)):

        @pl.when(there)
        def _():
            pl.semaphore_signal(barrier, inc=1, device_id={"ctx": t}, device_id_type=MESH)

    pl.semaphore_wait(barrier, 4 + jnp.where((x == 1) | (x == 2), 1, 0))

    def rc(src, dst, ss, rs, to):
        return pltpu.make_async_remote_copy(src_ref=src, dst_ref=dst, send_sem=ss, recv_sem=rs,
                                            device_id={"ctx": to}, device_id_type=MESH)

    def block(h, kind, slot):
        return kv.at[h, kind, pl.ds(slot * R, R)]

    def part(slot):
        return pl.ds(slot * R, R)

    def routes(h, kind):
        def one(num, src_slot, slot, to):
            return rc(block(h, kind, src_slot), block(h, kind, slot), gs.at[h, kind, num], gr.at[h, kind, slot], to)

        return {
            0: (x < 3, lambda: one(0, 8, 4, me + 4)),
            1: (yl == 0, lambda: one(1, 8, 6, ypar)),
            2: (c == 0, lambda: one(2, 8, 7, core)),
            3: (x < 2, lambda: one(3, 8, 0, me + 8)),
            4: (x > 0, lambda: one(4, 4, 2 + 4 * yl, ypar)),
            5: (x > 0, lambda: one(5, 4, 3 + 2 * c, core)),
            6: (me >= 2, lambda: one(6, 6, 5 + 2 * c, core)),
            7: ((x > 1) & (yl == 1), lambda: one(7, 0, 2, ypar)),
            8: ((x > 1) & (c == 1), lambda: one(8, 0, 1, core)),
            9: (me >= 6, lambda: one(9, 2, 1 + 2 * c, core)),
        }

    def go(h, nums):
        for kind in range(2):
            r = routes(h, kind)
            for n in nums:
                pl.when(r[n][0])(lambda n=n, r=r: r[n][1]().start())

    def arrived(h, kind, slot):
        @pl.when(me >= 8 - slot)
        def _():
            rc(block(h, kind, slot), block(h, kind, slot), gs.at[h, kind, 0], gr.at[h, kind, slot], core).wait_recv()

    def after(h, slot, nums):
        for kind in range(2):
            arrived(h, kind, slot)
            r = routes(h, kind)
            for n in nums:
                pl.when(r[n][0])(lambda n=n, r=r: r[n][1]().start())

    def odd_slots(h):
        for kind in range(2):
            for slot in (7, 5, 3, 1):
                arrived(h, kind, slot)

    def core_copy(h, kind, j):
        return rc(cs.at[h, kind, j], cr.at[h, kind, j], css.at[h, kind, j], crs.at[h, kind, j], core)

    def y_copy(h, kind, j):
        return rc(ys.at[h, kind, j], yr.at[h, kind, j], yss.at[h, kind, j], yrs.at[h, kind, j], ypar)

    def x_copy(h, kind, j):
        return rc(xs.at[h, kind, j], xr.at[h, kind, j], xss.at[h, kind, j], xrs.at[h, kind, j], me - 8 + 4 * j)

    def core_send(h):
        for j in (3, 2, 0, 1):
            @pl.when(me >= 2 * j + 1)
            def _():
                for kind in (1, 0):
                    cs[h, kind, j] = dkv[h, kind, part(7 - 2 * j), :].astype(BF)
                    core_copy(h, kind, j).start()

    def core_add(h, kind, j):
        @pl.when(core >= 2 * j + 1)
        def _():
            core_copy(h, kind, j).wait_recv()
            to = 8 - 2 * j - 2 * c
            dkv[h, kind, part(to), :] += cr[h, kind, j].astype(F32)

    def y_send(h, kind, j):
        @pl.when(me >= 2 + 4 * j)
        def _():
            ys[h, kind, j] = dkv[h, kind, part(6 - 4 * j), :].astype(BF)
            y_copy(h, kind, j).start()

    def y_add(h, kind, j):
        @pl.when(ypar >= 2 + 4 * j)
        def _():
            y_copy(h, kind, j).wait_recv()
            to = 8 - 4 * (j + yl)
            dkv[h, kind, part(to), :] += yr[h, kind, j].astype(F32)

    def x_send(h, kind, j):
        @pl.when(x >= 2 - j)
        def _():
            xs[h, kind, j] = dkv[h, kind, part(4 * j), :].astype(BF)
            x_copy(h, kind, j).start()

    def x_add(h, kind, j):
        @pl.when(x <= 1 + j)
        def _():
            x_copy(h, kind, j).wait_recv()
            dkv[h, kind, part(8), :] += xr[h, kind, j].astype(F32)

    def red1(h):
        for kind in (1, 0):
            core_add(h, kind, 3)
            core_add(h, kind, 2)
            y_send(h, kind, 1)
            pl.when(yl == 0)(lambda: x_send(h, kind, 0))
        for kind in (1, 0):
            core_add(h, kind, 0)
            core_add(h, kind, 1)
            y_send(h, kind, 0)

    def red2(h):
        for kind in (1, 0):
            y_add(h, kind, 1)
            pl.when(yl == 0)(lambda: x_send(h, kind, 1))
            pl.when(yl == 1)(lambda: x_send(h, kind, 0))

    def red3(h):
        for kind in (1, 0):
            y_add(h, kind, 0)
            pl.when(yl == 1)(lambda: x_send(h, kind, 1))

    def red4(h):
        for kind in (1, 0):
            x_add(h, kind, 0)
            x_add(h, kind, 1)
            t = dkv[h, kind, part(8), :]
            (gk, gv)[kind][pl.ds(h, R, stride=2), :] = t

    go(0, (0, 1, 2))
    go(0, (3,))

    for slot in range(8):
        @pl.when(me < 8 - slot)
        def _():
            for h in range(H):
                for kind in range(2):
                    kv[h, kind, part(slot), :] = jnp.zeros((R, D), BF)
    row = base + lax.broadcasted_iota(jnp.int32, (1, R), 1)
    first = bs[...]
    for half in range(2):
        sl = slice(half * 128, half * 128 + 128)

        def body(i, _):
            key = base - W + half * 128 + i * CH + lax.broadcasted_iota(jnp.int32, (CH, 128), 0)
            ok = (key >= first[:, sl]) & (key <= row[:, sl])
            bias[half, pl.ds(pl.multiple_of(i * CH, CH), CH), :] = jnp.where(ok, 0.0, NEG)
            return 0

        lax.fori_loop(0, NC, body, 0)

    def unpack(n, src, dst):
        loads[n].wait()
        tmp[...] = src[...].astype(F32)

        def body(g, _):
            for h in range(H):
                dst[h, g] = tmp[pl.ds(g * 2 + h, R, stride=24), :].astype(BF)
            return 0

        lax.fori_loop(0, G, body, 0)

    unpack(0, dqo, qs)
    after(0, 4, (4, 5))
    unpack(1, dov, dos)
    dkv[...] = jnp.zeros_like(dkv)
    after(0, 6, (6,))
    after(0, 0, (7, 8))
    after(0, 2, (9,))
    odd_slots(0)

    together(stage_a(0, 0, 0, qs, dos, kv, bias, p0, dp0, st0))

    steps = {
        0: lambda: go(1, (0, 1, 2, 3)),
        1: lambda: after(1, 4, (4, 5)),
        2: lambda: after(1, 6, (6,)),
        3: lambda: after(1, 0, (7, 8)),
        4: lambda: after(1, 2, (9,)),
        5: lambda: odd_slots(1),
        6: lambda: core_send(0),
        7: lambda: red1(0),
        9: lambda: red2(0),
        10: lambda: red3(0),
        11: lambda: red4(0),
    }

    def unit(it, _):
        for k, f in steps.items():
            pl.when(it == k)(f)
        h = it // 6
        gp = it % 6
        nx = jnp.minimum(it + 1, 11)
        together(
            stage_a(h, gp, 1, qs, dos, kv, bias, p1, dp1, st1), stage_b(h, gp, 0, qs, dos, p0, dp0, st0, dkv, dss)
        )
        together(
            stage_a(nx // 6, nx % 6, 0, qs, dos, kv, bias, p0, dp0, st0),
            stage_b(h, gp, 1, qs, dos, p1, dp1, st1, dkv, dss),
        )
        return 0

    lax.fori_loop(0, 12, unit, 0)
    def out_copy(half):
        rows = pl.ds(half * R * 12, R * 12)
        return pltpu.make_async_copy(dqo.at[rows], dq.at[rows], lsem.at[half])

    def put_out(half):
        rows = slice(half * R * 12, (half + 1) * R * 12)
        dqo[rows] = tmp[rows].astype(BF)
        out_copy(half).start()

    core_send(1)
    for h in range(H):
        kt[h] = kv[h, 0].T
    query_gradients(0, 0, 4, kt, dss, tmp)
    red1(1)
    query_gradients(0, 4, 12, kt, dss, tmp)
    put_out(0)
    red2(1)
    query_gradients(1, 0, 6, kt, dss, tmp)
    red3(1)
    query_gradients(1, 6, 12, kt, dss, tmp)
    put_out(1)
    red4(1)
    for half in range(2):
        out_copy(half).wait()
    for h in range(H):
        for kind in range(2):
            r = routes(h, kind)
            for n in range(10):
                pl.when(r[n][0])(lambda n=n, r=r: r[n][1]().wait_send())
            for j in range(4):
                pl.when(me >= 2 * j + 1)(lambda h=h, kind=kind, j=j: core_copy(h, kind, j).wait_send())
            for j in range(2):
                pl.when(me >= 2 + 4 * j)(lambda h=h, kind=kind, j=j: y_copy(h, kind, j).wait_send())
                pl.when(x >= 2 - j)(lambda h=h, kind=kind, j=j: x_copy(h, kind, j).wait_send())


def fused(q2, do2, k2, v2, bs):
    vm = pl.BlockSpec(memory_space=pltpu.VMEM)
    hbm = pl.BlockSpec(memory_space=pl.ANY)
    tile = pltpu.VMEM((KW // 8, 8, 256), F32)
    stats = pltpu.VMEM((len(chunks()) + 1, 8, 256), F32)
    dma = pltpu.SemaphoreType.DMA
    return pl.pallas_call(
        kernel,
        out_shape=(jax.ShapeDtypeStruct((R * 24, D), BF), jax.ShapeDtypeStruct((R * 2, D), F32),
                   jax.ShapeDtypeStruct((R * 2, D), F32)),
        in_specs=[hbm, hbm, vm, vm, vm],
        out_specs=(hbm, vm, vm),
        scratch_shapes=[
            pltpu.VMEM((R * 24, D), BF), pltpu.VMEM((R * 24, D), BF), pltpu.VMEM((24, KW, 256), BF),
            pltpu.VMEM((H, G, R, D), BF), pltpu.VMEM((H, G, R, D), BF),
            pltpu.VMEM((R * 24, D), F32), pltpu.VMEM((2, KW, 128), F32),
            pltpu.VMEM((H, 2, W + R, D), BF), pltpu.VMEM((H, D, W + R), BF), pltpu.VMEM((H, 2, W + R, D), F32),
            tile, tile, stats, tile, tile, stats,
            pltpu.VMEM((H, 2, 4, R, D), BF), pltpu.VMEM((H, 2, 4, R, D), BF),
            pltpu.VMEM((H, 2, 2, R, D), BF), pltpu.VMEM((H, 2, 2, R, D), BF),
            pltpu.VMEM((H, 2, 2, R, D), BF), pltpu.VMEM((H, 2, 2, R, D), BF),
            dma((2,)), dma((H, 2, 10)), dma((H, 2, 9)),
            dma((H, 2, 4)), dma((H, 2, 4)), dma((H, 2, 2)), dma((H, 2, 2)), dma((H, 2, 2)), dma((H, 2, 2)),
        ],
        compiler_params=pltpu.CompilerParams(collective_id=0, has_side_effects=True, vmem_limit_bytes=VLIM),
    )(q2, do2, k2, v2, bs)


def finish_kernel(dq, gk, gv, dq_out, gk_out, gv_out):
    dq_out[...] = dq[...].astype(F32) * SC
    gk_out[...] = gk[...] * SC
    gv_out[...] = gv[...]


def finish(dq, gk, gv):
    n = 4
    specs = [pl.BlockSpec((r // n, D), lambda i: (i, 0)) for r in (R * 24, R * 2, R * 2)]
    return pl.pallas_call(
        finish_kernel,
        grid=(n,),
        out_shape=[jax.ShapeDtypeStruct(a.shape, F32) for a in (dq, gk, gv)],
        in_specs=specs,
        out_specs=specs,
    )(dq, gk, gv)


def shards(queries, keys, values, output_gradient, band_start):
    q2 = queries.transpose(0, 2, 1, 3).reshape(R * 24, D)
    d2 = output_gradient.transpose(0, 2, 1, 3).reshape(R * 24, D)
    dq, gk, gv = fused(q2, d2, keys.reshape(R * H, D), values.reshape(R * H, D), band_start.reshape(1, R))
    dq, gk, gv = finish(dq, gk, gv)
    return dq.reshape(R, G, H, D).transpose(0, 2, 1, 3), gk.reshape(R, H, D), gv.reshape(R, H, D)


def solution(mesh):
    rows = P(("rep", "ctx"), "kv", None, None)
    keyed = P(("rep", "ctx"), "kv", None)
    return jax.shard_map(shards, mesh=mesh, in_specs=(rows, keyed, keyed, rows, P(("rep", "ctx"))),
                         out_specs=(rows, keyed, keyed), check_vma=False)
```

```python
import functools, math
import jax, jax.numpy as jnp
from jax import lax
from jax.experimental import pallas as pl
from jax.experimental.pallas import tpu as pltpu
from jax.sharding import PartitionSpec as P

R = 256
G = 12
H = 2
D = 128
W = 2048
CH = 128
SZ = 512
KW = W + 128
NC = KW // CH
NB = W // R
SC = D**-0.5
C2 = SC * math.log2(math.e)
NEG = -1e30
VLIM = 63 * 2**20
NT = (((1,), (1,)), ((), ()))
NN = (((1,), (0,)), ((), ()))
TN = (((0,), (0,)), ((), ()))
MESH = pl.DeviceIdType.MESH
BF = jnp.bfloat16
F32 = jnp.float32


def dot(a, b, dims):
    return lax.dot_general(a, b, dims, preferred_element_type=F32)


def chunks():
    return [(o, min(SZ, KW - o)) for o in range(0, KW, SZ)]


def unit_rows(ref, h, gp, half):
    return ref[h, pl.ds(gp * 2, 2), half * 128 : half * 128 + 128, :].reshape(256, D)


def stage_a(h, gp, half, qs, dos, kv, bias, p, dp, st, backwards=False):
    qu = unit_rows(qs, h, gp, half)
    du = unit_rows(dos, h, gp, half)
    m = jnp.full((1, 8, 256), NEG, F32)
    l = jnp.zeros((1, 8, 256), F32)
    dd = l
    numbered = list(enumerate(chunks()))
    for i, (o, n) in numbered[::-1] if backwards else numbered:
        keys = slice(half * 128 + o, half * 128 + o + n)
        s = dot(kv[h, 0, keys, :], qu, NT) * C2
        g = dot(kv[h, 1, keys, :], du, NT)
        b = bias[half, o : o + n, :]
        s = (s + jnp.concatenate([b, b], 1)).reshape(n // 8, 8, 256)
        g = g.reshape(n // 8, 8, 256)
        mn = jnp.maximum(m, jnp.max(s, 0, keepdims=True))
        al = jnp.exp2(m - mn)
        e = jnp.exp2(s - mn)
        l = l * al + jnp.sum(e, 0, keepdims=True)
        dd = dd * al + jnp.sum(e * g, 0, keepdims=True)
        p[o // 8 : (o + n) // 8] = e
        dp[o // 8 : (o + n) // 8] = g
        st[i] = mn[0]
        m = mn
        yield 1
    mm = jnp.max(m, 1, keepdims=True)
    e = jnp.exp2(m - mm)
    il = 1.0 / jnp.sum(l * e, 1, keepdims=True)
    ds = jnp.sum(dd * e, 1, keepdims=True) * il
    nc = len(chunks())
    for i in range(nc):
        st[i] = jnp.exp2(st[i] - mm[0]) * il[0]
    st[nc] = jnp.broadcast_to(ds[0], (8, 256))
    yield 1


def stage_b(h, gp, half, qs, dos, p, dp, st, dkv, dss):
    qu = unit_rows(qs, h, gp, half)
    du = unit_rows(dos, h, gp, half)
    dsum = st[len(chunks())][None]
    u = (h * 6 + gp) * 2 + half
    for i, (o, n) in enumerate(chunks()):
        keys = slice(half * 128 + o, half * 128 + o + n)
        w = p[o // 8 : (o + n) // 8] * st[i][None]
        x = w * (dp[o // 8 : (o + n) // 8] - dsum)
        wb = w.reshape(n, 256).astype(BF)
        xb = x.reshape(n, 256).astype(BF)
        dkv[h, 1, keys, :] += dot(wb, du, NN)
        dkv[h, 0, keys, :] += dot(xb, qu, NN)
        dss[u, o : o + n, :] = xb
        yield 1


def query_gradients(half, first, last, kt, dss, dq):
    def body(it, _):
        h = it // 6
        gp = it % 6
        t = dot(kt[h, :, half * 128 : half * 128 + KW], dss[it * 2 + half], NN).T
        for i in range(2):
            dq[pl.ds(half * 128 * 24 + (gp * 2 + i) * 2 + h, 128, stride=24), :] = t[i * 128 : (i + 1) * 128]
        return 0

    lax.fori_loop(first, last, body, 0)


def together(*steps):
    steps = list(steps)
    while steps:
        for s in list(steps):
            if next(s, 0) == 0:
                steps.remove(s)


def kernel(q2, do2, k2, v2, bs, dq, gk, gv, dqo, dov, dss, qs, dos, tmp, bias, kvin, first, kv, kt, dkv, p0, dp0, st0, p1, dp1, st1,
           cs, cr, ys, yr, xs, xr, lsem, gs, gr, css, crs, yss, yrs, xss, xrs):
    me = lax.axis_index("ctx")
    x = me // 4
    yl = (me // 2) % 2
    c = me % 2
    base = me * R
    core = me + 1 - 2 * c
    ypar = me + 2 - 4 * yl

    own = [
        pltpu.make_async_copy(k2, kvin.at[0], lsem.at[2]),
        pltpu.make_async_copy(v2, kvin.at[1], lsem.at[3]),
        pltpu.make_async_copy(bs, first, lsem.at[4]),
    ]
    for a in own:
        a.start()
    loads = [pltpu.make_async_copy(q2, dqo, lsem.at[0]), pltpu.make_async_copy(do2, dov, lsem.at[1])]
    for a in loads:
        a.start()

    barrier = pltpu.get_barrier_semaphore()
    for t in (core, ypar):
        pl.semaphore_signal(barrier, inc=1, device_id={"ctx": t}, device_id_type=MESH)

    for there, t in ((x < 3, me + 4), (x > 0, me - 4), (x < 2, me + 8), (x > 1, me - 8)):

        @pl.when(there)
        def _():
            pl.semaphore_signal(barrier, inc=1, device_id={"ctx": t}, device_id_type=MESH)

    for kind in range(2):
        own[kind].wait()
        tmp[kind * 2 * R : (kind + 1) * 2 * R] = kvin[kind].astype(F32)
        for h in range(H):
            kv[h, kind, NB * R :] = tmp[pl.ds(kind * 2 * R + h, R, stride=2), :].astype(BF)

    pl.semaphore_wait(barrier, 4 + jnp.where((x == 1) | (x == 2), 1, 0))

    def rc(src, dst, ss, rs, to):
        return pltpu.make_async_remote_copy(src_ref=src, dst_ref=dst, send_sem=ss, recv_sem=rs,
                                            device_id={"ctx": to}, device_id_type=MESH)

    def block(h, kind, slot):
        return kv.at[h, kind, pl.ds(slot * R, R)]

    def part(slot):
        return pl.ds(slot * R, R)

    def routes(h, kind):
        def one(num, src_slot, slot, to):
            return rc(block(h, kind, src_slot), block(h, kind, slot), gs.at[h, kind, num], gr.at[h, kind, slot], to)

        return {
            0: (x < 3, lambda: one(0, 8, 4, me + 4)),
            1: (yl == 0, lambda: one(1, 8, 6, ypar)),
            2: (c == 0, lambda: one(2, 8, 7, core)),
            3: (x < 2, lambda: one(3, 8, 0, me + 8)),
            4: (x > 0, lambda: one(4, 4, 2 + 4 * yl, ypar)),
            5: (x > 0, lambda: one(5, 4, 3 + 2 * c, core)),
            6: (me >= 2, lambda: one(6, 6, 5 + 2 * c, core)),
            7: ((x > 1) & (yl == 1), lambda: one(7, 0, 2, ypar)),
            8: ((x > 1) & (c == 1), lambda: one(8, 0, 1, core)),
            9: (me >= 6, lambda: one(9, 2, 1 + 2 * c, core)),
        }

    def go(h, nums):
        for kind in range(2):
            r = routes(h, kind)
            for n in nums:
                pl.when(r[n][0])(lambda n=n, r=r: r[n][1]().start())

    def arrived(h, kind, slot):
        @pl.when(me >= 8 - slot)
        def _():
            rc(block(h, kind, slot), block(h, kind, slot), gs.at[h, kind, 0], gr.at[h, kind, slot], core).wait_recv()

    def after(h, slot, nums):
        for kind in range(2):
            arrived(h, kind, slot)
            r = routes(h, kind)
            for n in nums:
                pl.when(r[n][0])(lambda n=n, r=r: r[n][1]().start())

    def odd_slots(h):
        for kind in range(2):
            for slot in (7, 5, 3, 1):
                arrived(h, kind, slot)

    def core_copy(h, kind, j):
        return rc(cs.at[h, kind, j], cr.at[h, kind, j], css.at[h, kind, j], crs.at[h, kind, j], core)

    def y_copy(h, kind, j):
        return rc(ys.at[h, kind, j], yr.at[h, kind, j], yss.at[h, kind, j], yrs.at[h, kind, j], ypar)

    def x_copy(h, kind, j):
        return rc(xs.at[h, kind, j], xr.at[h, kind, j], xss.at[h, kind, j], xrs.at[h, kind, j], me - 8 + 4 * j)

    def core_send(h):
        for j in (3, 2, 0, 1):
            @pl.when(me >= 2 * j + 1)
            def _():
                for kind in (1, 0):
                    cs[h, kind, j] = dkv[h, kind, part(7 - 2 * j), :].astype(BF)
                    core_copy(h, kind, j).start()

    def core_add(h, kind, j):
        @pl.when(core >= 2 * j + 1)
        def _():
            core_copy(h, kind, j).wait_recv()
            to = 8 - 2 * j - 2 * c
            dkv[h, kind, part(to), :] += cr[h, kind, j].astype(F32)

    def y_send(h, kind, j):
        @pl.when(me >= 2 + 4 * j)
        def _():
            ys[h, kind, j] = dkv[h, kind, part(6 - 4 * j), :].astype(BF)
            y_copy(h, kind, j).start()

    def y_add(h, kind, j):
        @pl.when(ypar >= 2 + 4 * j)
        def _():
            y_copy(h, kind, j).wait_recv()
            to = 8 - 4 * (j + yl)
            dkv[h, kind, part(to), :] += yr[h, kind, j].astype(F32)

    def x_send(h, kind, j):
        @pl.when(x >= 2 - j)
        def _():
            xs[h, kind, j] = dkv[h, kind, part(4 * j), :].astype(BF)
            x_copy(h, kind, j).start()

    def x_add(h, kind, j):
        @pl.when(x <= 1 + j)
        def _():
            x_copy(h, kind, j).wait_recv()
            dkv[h, kind, part(8), :] += xr[h, kind, j].astype(F32)

    def red1(h):
        for kind in (1, 0):
            core_add(h, kind, 3)
            core_add(h, kind, 2)
            y_send(h, kind, 1)
            pl.when(yl == 0)(lambda: x_send(h, kind, 0))
        for kind in (1, 0):
            core_add(h, kind, 0)
            core_add(h, kind, 1)
            y_send(h, kind, 0)

    def red2(h):
        for kind in (1, 0):
            y_add(h, kind, 1)
            pl.when(yl == 0)(lambda: x_send(h, kind, 1))
            pl.when(yl == 1)(lambda: x_send(h, kind, 0))

    def red3(h):
        for kind in (1, 0):
            y_add(h, kind, 0)
            pl.when(yl == 1)(lambda: x_send(h, kind, 1))

    def red4(h):
        for kind in (1, 0):
            x_add(h, kind, 0)
            x_add(h, kind, 1)
            t = dkv[h, kind, part(8), :]
            (gk, gv)[kind][pl.ds(h, R, stride=2), :] = t

    go(0, (0, 1, 2))
    go(0, (3,))

    for slot in range(8):
        @pl.when(me < 8 - slot)
        def _():
            for h in range(H):
                for kind in range(2):
                    kv[h, kind, part(slot), :] = jnp.zeros((R, D), BF)
    row = base + lax.broadcasted_iota(jnp.int32, (1, R), 1)
    own[2].wait()
    start = first[...]
    for half in range(2):
        sl = slice(half * 128, half * 128 + 128)

        def body(i, _):
            key = base - W + half * 128 + i * CH + lax.broadcasted_iota(jnp.int32, (CH, 128), 0)
            ok = (key >= start[:, sl]) & (key <= row[:, sl])
            bias[half, pl.ds(pl.multiple_of(i * CH, CH), CH), :] = jnp.where(ok, 0.0, NEG)
            return 0

        lax.fori_loop(0, NC, body, 0)

    def unpack(n, src, dst):
        loads[n].wait()
        tmp[...] = src[...].astype(F32)

        def body(g, _):
            for h in range(H):
                dst[h, g] = tmp[pl.ds(g * 2 + h, R, stride=24), :].astype(BF)
            return 0

        lax.fori_loop(0, G, body, 0)

    unpack(0, dqo, qs)
    after(0, 4, (4, 5))
    unpack(1, dov, dos)
    dkv[...] = jnp.zeros_like(dkv)
    after(0, 6, (6,))
    opening = stage_a(0, 0, 0, qs, dos, kv, bias, p0, dp0, st0, backwards=True)
    next(opening)
    for slot, nums, odd in ((6, None, 7), (0, (7, 8), 5), (2, (9,), 3), (None, None, 1)):
        if nums:
            after(0, slot, nums)
        for kind in range(2):
            arrived(0, kind, odd)
        next(opening)
    together(opening)

    steps = {
        0: lambda: go(1, (0, 1, 2, 3)),
        1: lambda: after(1, 4, (4, 5)),
        2: lambda: after(1, 6, (6,)),
        3: lambda: after(1, 0, (7, 8)),
        4: lambda: after(1, 2, (9,)),
        5: lambda: odd_slots(1),
        6: lambda: core_send(0),
        7: lambda: red1(0),
        9: lambda: red2(0),
        10: lambda: red3(0),
        11: lambda: red4(0),
    }

    def unit(it, _):
        for k, f in steps.items():
            pl.when(it == k)(f)
        h = it // 6
        gp = it % 6
        nx = jnp.minimum(it + 1, 11)
        together(
            stage_a(h, gp, 1, qs, dos, kv, bias, p1, dp1, st1), stage_b(h, gp, 0, qs, dos, p0, dp0, st0, dkv, dss)
        )
        together(
            stage_a(nx // 6, nx % 6, 0, qs, dos, kv, bias, p0, dp0, st0),
            stage_b(h, gp, 1, qs, dos, p1, dp1, st1, dkv, dss),
        )
        return 0

    lax.fori_loop(0, 12, unit, 0)
    def out_copy(half):
        rows = pl.ds(half * R * 12, R * 12)
        return pltpu.make_async_copy(dqo.at[rows], dq.at[rows], lsem.at[half])

    def put_out(half):
        rows = slice(half * R * 12, (half + 1) * R * 12)
        dqo[rows] = tmp[rows].astype(BF)
        out_copy(half).start()

    core_send(1)
    for h in range(H):
        kt[h] = kv[h, 0].T
    query_gradients(0, 0, 4, kt, dss, tmp)
    red1(1)
    query_gradients(0, 4, 12, kt, dss, tmp)
    put_out(0)
    red2(1)
    query_gradients(1, 0, 6, kt, dss, tmp)
    red3(1)
    query_gradients(1, 6, 12, kt, dss, tmp)
    put_out(1)
    red4(1)
    for half in range(2):
        out_copy(half).wait()
    for h in range(H):
        for kind in range(2):
            r = routes(h, kind)
            for n in range(10):
                pl.when(r[n][0])(lambda n=n, r=r: r[n][1]().wait_send())
            for j in range(4):
                pl.when(me >= 2 * j + 1)(lambda h=h, kind=kind, j=j: core_copy(h, kind, j).wait_send())
            for j in range(2):
                pl.when(me >= 2 + 4 * j)(lambda h=h, kind=kind, j=j: y_copy(h, kind, j).wait_send())
                pl.when(x >= 2 - j)(lambda h=h, kind=kind, j=j: x_copy(h, kind, j).wait_send())


def fused(q2, do2, k2, v2, bs):
    vm = pl.BlockSpec(memory_space=pltpu.VMEM)
    hbm = pl.BlockSpec(memory_space=pl.ANY)
    tile = pltpu.VMEM((KW // 8, 8, 256), F32)
    stats = pltpu.VMEM((len(chunks()) + 1, 8, 256), F32)
    dma = pltpu.SemaphoreType.DMA
    return pl.pallas_call(
        kernel,
        out_shape=(jax.ShapeDtypeStruct((R * 24, D), BF), jax.ShapeDtypeStruct((R * 2, D), F32),
                   jax.ShapeDtypeStruct((R * 2, D), F32)),
        in_specs=[hbm] * 5,
        out_specs=(hbm, vm, vm),
        scratch_shapes=[
            pltpu.VMEM((R * 24, D), BF), pltpu.VMEM((R * 24, D), BF), pltpu.VMEM((24, KW, 256), BF),
            pltpu.VMEM((H, G, R, D), BF), pltpu.VMEM((H, G, R, D), BF),
            pltpu.VMEM((R * 24, D), F32), pltpu.VMEM((2, KW, 128), F32),
            pltpu.VMEM((2, R * H, D), BF), pltpu.VMEM((1, R), jnp.int32),
            pltpu.VMEM((H, 2, W + R, D), BF), pltpu.VMEM((H, D, W + R), BF), pltpu.VMEM((H, 2, W + R, D), F32),
            tile, tile, stats, tile, tile, stats,
            pltpu.VMEM((H, 2, 4, R, D), BF), pltpu.VMEM((H, 2, 4, R, D), BF),
            pltpu.VMEM((H, 2, 2, R, D), BF), pltpu.VMEM((H, 2, 2, R, D), BF),
            pltpu.VMEM((H, 2, 2, R, D), BF), pltpu.VMEM((H, 2, 2, R, D), BF),
            dma((5,)), dma((H, 2, 10)), dma((H, 2, 9)),
            dma((H, 2, 4)), dma((H, 2, 4)), dma((H, 2, 2)), dma((H, 2, 2)), dma((H, 2, 2)), dma((H, 2, 2)),
        ],
        compiler_params=pltpu.CompilerParams(collective_id=0, has_side_effects=True, vmem_limit_bytes=VLIM),
    )(q2, do2, k2, v2, bs)


def finish_kernel(dq, gk, gv, dq_out, gk_out, gv_out, narrow, wide, kin, sin, sout):
    n = 4
    rows = R * 24 // n
    ins = [pltpu.make_async_copy(dq.at[pl.ds(i * rows, rows)], narrow.at[i], sin.at[i]) for i in range(n)]
    ins += [pltpu.make_async_copy(src, kin.at[i], sin.at[n + i]) for i, src in enumerate((gk, gv))]
    outs = [pltpu.make_async_copy(wide.at[i], dq_out.at[pl.ds(i * rows, rows)], sout.at[i]) for i in range(n)]
    outs += [pltpu.make_async_copy(kin.at[2], gk_out, sout.at[n]), pltpu.make_async_copy(kin.at[1], gv_out, sout.at[n + 1])]
    for a in ins:
        a.start()
    for i in range(n):
        ins[i].wait()
        wide[i] = narrow[i].astype(F32) * SC
        outs[i].start()
    ins[n].wait()
    kin[2] = kin[0] * SC
    outs[n].start()
    ins[n + 1].wait()
    outs[n + 1].start()
    for a in outs:
        a.wait()


def finish(dq, gk, gv):
    n = 4
    hbm = pl.BlockSpec(memory_space=pl.ANY)
    return pl.pallas_call(
        finish_kernel,
        out_shape=[jax.ShapeDtypeStruct(a.shape, F32) for a in (dq, gk, gv)],
        in_specs=[hbm] * 3,
        out_specs=[hbm] * 3,
        scratch_shapes=[
            pltpu.VMEM((n, R * 24 // n, D), BF), pltpu.VMEM((n, R * 24 // n, D), F32), pltpu.VMEM((3, R * 2, D), F32),
            pltpu.SemaphoreType.DMA((n + 2,)), pltpu.SemaphoreType.DMA((n + 2,)),
        ],
        compiler_params=pltpu.CompilerParams(vmem_limit_bytes=62 * 2**20),
    )(dq, gk, gv)


def shards(queries, keys, values, output_gradient, band_start):
    q2 = queries.transpose(0, 2, 1, 3).reshape(R * 24, D)
    d2 = output_gradient.transpose(0, 2, 1, 3).reshape(R * 24, D)
    dq, gk, gv = fused(q2, d2, keys.reshape(R * H, D), values.reshape(R * H, D), band_start.reshape(1, R))
    dq, gk, gv = finish(dq, gk, gv)
    return dq.reshape(R, G, H, D).transpose(0, 2, 1, 3), gk.reshape(R, H, D), gv.reshape(R, H, D)


def solution(mesh):
    rows = P(("rep", "ctx"), "kv", None, None)
    keyed = P(("rep", "ctx"), "kv", None)
    return jax.shard_map(shards, mesh=mesh, in_specs=(rows, keyed, keyed, rows, P(("rep", "ctx"))),
                         out_specs=(rows, keyed, keyed), check_vma=False)
```

```python
import functools, math
import jax, jax.numpy as jnp
from jax import lax
from jax.experimental import pallas as pl
from jax.experimental.pallas import tpu as pltpu
from jax.sharding import PartitionSpec as P

R = 256
G = 12
H = 2
D = 128
W = 2048
CH = 128
SZ = 352
QT = 64
KW = W + QT
KP = W + 128
NB = W // R
SC = D**-0.5
C2 = SC * math.log2(math.e)
NEG = -1e30
VLIM = 63 * 2**20
NT = (((1,), (1,)), ((), ()))
NN = (((1,), (0,)), ((), ()))
TN = (((0,), (0,)), ((), ()))
MESH = pl.DeviceIdType.MESH
BF = jnp.bfloat16
F32 = jnp.float32


def dot(a, b, dims):
    return lax.dot_general(a, b, dims, preferred_element_type=F32)


def chunks():
    return [(o, min(SZ, KW - o)) for o in range(0, KW, SZ)]


def unit_rows(ref, h, gq, qt):
    return ref[h, pl.ds(gq * 4, 4), pl.ds(pl.multiple_of(qt * QT, QT), QT), :].reshape(256, D)


def unit_keys(qt, o, n):
    return pl.ds(pl.multiple_of(qt * QT + o, 16), n)


def stage_a(h, gq, qt, qs, dos, kv, bias, p, dp, st, backwards=False):
    qu = unit_rows(qs, h, gq, qt)
    du = unit_rows(dos, h, gq, qt)
    m = jnp.full((1, 8, 256), NEG, F32)
    l = jnp.zeros((1, 8, 256), F32)
    dd = l
    numbered = list(enumerate(chunks()))
    for i, (o, n) in numbered[::-1] if backwards else numbered:
        keys = unit_keys(qt, o, n)
        s = dot(kv[h, 0, keys, :], qu, NT) * C2
        g = dot(kv[h, 1, keys, :], du, NT)
        b = bias[qt, o : o + n, :]
        s = (s + jnp.concatenate([b, b], 1)).reshape(n // 8, 8, 256)
        g = g.reshape(n // 8, 8, 256)
        mn = jnp.maximum(m, jnp.max(s, 0, keepdims=True))
        al = jnp.exp2(m - mn)
        e = jnp.exp2(s - mn)
        l = l * al + jnp.sum(e, 0, keepdims=True)
        dd = dd * al + jnp.sum(e * g, 0, keepdims=True)
        p[o // 8 : (o + n) // 8] = e
        dp[o // 8 : (o + n) // 8] = g
        st[i] = mn[0]
        m = mn
        yield 1
    mm = jnp.max(m, 1, keepdims=True)
    e = jnp.exp2(m - mm)
    il = 1.0 / jnp.sum(l * e, 1, keepdims=True)
    ds = jnp.sum(dd * e, 1, keepdims=True) * il
    nc = len(chunks())
    for i in range(nc):
        st[i] = jnp.exp2(st[i] - mm[0]) * il[0]
    st[nc] = jnp.broadcast_to(ds[0], (8, 256))
    yield 1


def stage_b(h, gq, qt, u, pad, qs, dos, p, dp, st, dkv, dss):
    qu = unit_rows(qs, h, gq, qt)
    du = unit_rows(dos, h, gq, qt)
    dsum = st[len(chunks())][None]
    for i, (o, n) in enumerate(chunks()):
        keys = unit_keys(qt, o, n)
        w = p[o // 8 : (o + n) // 8] * st[i][None]
        x = w * (dp[o // 8 : (o + n) // 8] - dsum)
        wb = w.reshape(n, 256).astype(BF)
        xb = x.reshape(n, 256).astype(BF)
        dkv[h, 1, keys, :] += dot(wb, du, NN)
        dkv[h, 0, keys, :] += dot(xb, qu, NN)
        dss[u, pad + o : pad + o + n, :] = xb
        yield 1


def query_gradients(half, first, last, kt, dss, dq):
    def body(i, _):
        h = i // 3
        gq = i % 3
        u = (h * 6 + gq * 2 + half) * 2
        tiles = [kt[h, i // 2, i % 2 * 128 : i % 2 * 128 + 128, :] for i in range(half, half + KP // 128)]
        keys = jnp.concatenate(tiles, 1)
        for side in range(2):
            t = dot(keys, dss[u + side], NN).T
            for k in range(4):
                row = (half * 2 + side) * QT * 24 + (gq * 4 + k) * 2 + h
                dq[pl.ds(row, QT, stride=24), :] = t[k * QT : (k + 1) * QT]
        return 0

    lax.fori_loop(first, last, body, 0)


def together(*steps):
    steps = list(steps)
    while steps:
        for s in list(steps):
            if next(s, 0) == 0:
                steps.remove(s)


def kernel(q2, do2, k2, v2, bs, dq, gk, gv, dqo, dss, qs, dos, tmp, bias, kvin, first, kv, dkv, p0, dp0, st0, p1, dp1, st1,
           cs, cr, ys, yr, xs, xr, lsem, gs, gr, css, crs, yss, yrs, xss, xrs):
    me = lax.axis_index("ctx")
    x = me // 4
    yl = (me // 2) % 2
    c = me % 2
    base = me * R
    core = me + 1 - 2 * c
    ypar = me + 2 - 4 * yl

    own = [
        pltpu.make_async_copy(k2, kvin.at[0], lsem.at[2]),
        pltpu.make_async_copy(v2, kvin.at[1], lsem.at[3]),
        pltpu.make_async_copy(bs, first, lsem.at[4]),
    ]
    for a in own:
        a.start()
    loads = [pltpu.make_async_copy(q2, dqo, lsem.at[0]), pltpu.make_async_copy(do2, dqo, lsem.at[1])]
    loads[0].start()

    barrier = pltpu.get_barrier_semaphore()
    for t in (core, ypar):
        pl.semaphore_signal(barrier, inc=1, device_id={"ctx": t}, device_id_type=MESH)

    for there, t in ((x < 3, me + 4), (x > 0, me - 4), (x < 2, me + 8), (x > 1, me - 8)):

        @pl.when(there)
        def _():
            pl.semaphore_signal(barrier, inc=1, device_id={"ctx": t}, device_id_type=MESH)

    for kind in range(2):
        own[kind].wait()
        tmp[kind * 2 * R : (kind + 1) * 2 * R] = kvin[kind].astype(F32)
        for h in range(H):
            kv[h, kind, NB * R :] = tmp[pl.ds(kind * 2 * R + h, R, stride=2), :].astype(BF)

    pl.semaphore_wait(barrier, 4 + jnp.where((x == 1) | (x == 2), 1, 0))

    def rc(src, dst, ss, rs, to):
        return pltpu.make_async_remote_copy(src_ref=src, dst_ref=dst, send_sem=ss, recv_sem=rs,
                                            device_id={"ctx": to}, device_id_type=MESH)

    def block(h, kind, slot):
        return kv.at[h, kind, pl.ds(slot * R, R)]

    def part(slot):
        return pl.ds(slot * R, R)

    def routes(h, kind):
        def one(num, src_slot, slot, to):
            return rc(block(h, kind, src_slot), block(h, kind, slot), gs.at[h, kind, num], gr.at[h, kind, slot], to)

        return {
            0: (x < 3, lambda: one(0, 8, 4, me + 4)),
            1: (yl == 0, lambda: one(1, 8, 6, ypar)),
            2: (c == 0, lambda: one(2, 8, 7, core)),
            3: (x < 2, lambda: one(3, 8, 0, me + 8)),
            4: (x > 0, lambda: one(4, 4, 2 + 4 * yl, ypar)),
            5: (x > 0, lambda: one(5, 4, 3 + 2 * c, core)),
            6: (me >= 2, lambda: one(6, 6, 5 + 2 * c, core)),
            7: ((x > 1) & (yl == 1), lambda: one(7, 0, 2, ypar)),
            8: ((x > 1) & (c == 1), lambda: one(8, 0, 1, core)),
            9: (me >= 6, lambda: one(9, 2, 1 + 2 * c, core)),
        }

    def go(h, nums):
        for kind in range(2):
            r = routes(h, kind)
            for n in nums:
                pl.when(r[n][0])(lambda n=n, r=r: r[n][1]().start())

    def arrived(h, kind, slot):
        @pl.when(me >= 8 - slot)
        def _():
            rc(block(h, kind, slot), block(h, kind, slot), gs.at[h, kind, 0], gr.at[h, kind, slot], core).wait_recv()

    def after(h, slot, nums):
        for kind in range(2):
            arrived(h, kind, slot)
            r = routes(h, kind)
            for n in nums:
                pl.when(r[n][0])(lambda n=n, r=r: r[n][1]().start())

    def odd_slots(h):
        for kind in range(2):
            for slot in (7, 5, 3, 1):
                arrived(h, kind, slot)

    def core_copy(h, kind, j):
        return rc(cs.at[h, kind, j], cr.at[h, kind, j], css.at[h, kind, j], crs.at[h, kind, j], core)

    def y_copy(h, kind, j):
        return rc(ys.at[h, kind, j], yr.at[h, kind, j], yss.at[h, kind, j], yrs.at[h, kind, j], ypar)

    def x_copy(h, kind, j):
        return rc(xs.at[h, kind, j], xr.at[h, kind, j], xss.at[h, kind, j], xrs.at[h, kind, j], me - 8 + 4 * j)

    def core_send(h):
        for j in (3, 2, 0, 1):
            @pl.when(me >= 2 * j + 1)
            def _():
                for kind in (1, 0):
                    cs[h, kind, j] = dkv[h, kind, part(7 - 2 * j), :].astype(BF)
                    core_copy(h, kind, j).start()

    def core_add(h, kind, j):
        @pl.when(core >= 2 * j + 1)
        def _():
            core_copy(h, kind, j).wait_recv()
            to = 8 - 2 * j - 2 * c
            dkv[h, kind, part(to), :] += cr[h, kind, j].astype(F32)

    def y_send(h, kind, j):
        @pl.when(me >= 2 + 4 * j)
        def _():
            ys[h, kind, j] = dkv[h, kind, part(6 - 4 * j), :].astype(BF)
            y_copy(h, kind, j).start()

    def y_add(h, kind, j):
        @pl.when(ypar >= 2 + 4 * j)
        def _():
            y_copy(h, kind, j).wait_recv()
            to = 8 - 4 * (j + yl)
            dkv[h, kind, part(to), :] += yr[h, kind, j].astype(F32)

    def x_send(h, kind, j):
        @pl.when(x >= 2 - j)
        def _():
            xs[h, kind, j] = dkv[h, kind, part(4 * j), :].astype(BF)
            x_copy(h, kind, j).start()

    def x_add(h, kind, j):
        @pl.when(x <= 1 + j)
        def _():
            x_copy(h, kind, j).wait_recv()
            dkv[h, kind, part(8), :] += xr[h, kind, j].astype(F32)

    def red1(h):
        for kind in (1, 0):
            core_add(h, kind, 3)
            core_add(h, kind, 2)
            y_send(h, kind, 1)
            pl.when(yl == 0)(lambda: x_send(h, kind, 0))
        for kind in (1, 0):
            core_add(h, kind, 0)
            core_add(h, kind, 1)
            y_send(h, kind, 0)

    def red2(h):
        for kind in (1, 0):
            y_add(h, kind, 1)
            pl.when(yl == 0)(lambda: x_send(h, kind, 1))
            pl.when(yl == 1)(lambda: x_send(h, kind, 0))

    def red3(h):
        for kind in (1, 0):
            y_add(h, kind, 0)
            pl.when(yl == 1)(lambda: x_send(h, kind, 1))

    def red4(h):
        for kind in (1, 0):
            x_add(h, kind, 0)
            x_add(h, kind, 1)
            t = dkv[h, kind, part(8), :]
            (gk, gv)[kind][pl.ds(h, R, stride=2), :] = t

    go(0, (0, 1, 2))
    go(0, (3,))

    for slot in range(8):
        @pl.when(me < 8 - slot)
        def _():
            for h in range(H):
                for kind in range(2):
                    kv[h, kind, part(slot), :] = jnp.zeros((R, D), BF)
    row = base + lax.broadcasted_iota(jnp.int32, (1, R), 1)
    own[2].wait()
    start = first[...]
    for qt in range(4):
        sl = slice(qt * QT, qt * QT + QT)
        low = jnp.concatenate([start[:, sl]] * 2, 1)
        high = jnp.concatenate([row[:, sl]] * 2, 1)

        def body(i, _):
            key = base - W + qt * QT + i * QT + lax.broadcasted_iota(jnp.int32, (QT, 128), 0)
            ok = (key >= low) & (key <= high)
            bias[qt, pl.ds(pl.multiple_of(i * QT, QT), QT), :] = jnp.where(ok, 0.0, NEG)
            return 0

        lax.fori_loop(0, KW // QT, body, 0)
    for u in range(0, 24, 2):
        dss[u, KW:, :] = jnp.zeros((QT, 256), BF)
        dss[u + 1, :QT, :] = jnp.zeros((QT, 256), BF)

    def unpack(n, src, dst):
        loads[n].wait()
        tmp[...] = src[...].astype(F32)
        if n == 0:
            loads[1].start()

        def body(g, _):
            for h in range(H):
                dst[h, g] = tmp[pl.ds(g * 2 + h, R, stride=24), :].astype(BF)
            return 0

        lax.fori_loop(0, G, body, 0)

    unpack(0, dqo, qs)
    after(0, 4, (4, 5))
    unpack(1, dqo, dos)
    dkv[...] = jnp.zeros_like(dkv)
    after(0, 6, (6,))
    opening = stage_a(0, 0, 0, qs, dos, kv, bias, p0, dp0, st0, backwards=True)
    for slot, nums, odd in ((6, None, 7), (0, (7, 8), 5), (2, (9,), 3), (None, None, 1)):
        if nums:
            after(0, slot, nums)
        for kind in range(2):
            arrived(0, kind, odd)
        next(opening)
    together(opening)

    steps = {
        0: lambda: go(1, (0, 1, 2, 3)),
        1: lambda: after(1, 4, (4, 5)),
        2: lambda: after(1, 6, (6,)),
        3: lambda: after(1, 0, (7, 8)),
        4: lambda: after(1, 2, (9,)),
        5: lambda: odd_slots(1),
        6: lambda: core_send(0),
        7: lambda: red1(0),
        9: lambda: red2(0),
        10: lambda: red3(0),
        11: lambda: red4(0),
    }

    def unit(it, _):
        for k, f in steps.items():
            pl.when(it == k)(f)
        def place(i):
            return i // 6, i % 6 // 2, i % 2 * 2

        h, gq, qt = place(it)
        h2, gq2, qt2 = place(jnp.minimum(it + 1, 11))
        together(
            stage_a(h, gq, qt + 1, qs, dos, kv, bias, p1, dp1, st1),
            stage_b(h, gq, qt, it * 2, 0, qs, dos, p0, dp0, st0, dkv, dss),
        )
        together(
            stage_a(h2, gq2, qt2, qs, dos, kv, bias, p0, dp0, st0),
            stage_b(h, gq, qt + 1, it * 2 + 1, QT, qs, dos, p1, dp1, st1, dkv, dss),
        )
        return 0

    lax.fori_loop(0, 12, unit, 0)
    def out_copy(half):
        rows = pl.ds(half * R * 12, R * 12)
        return pltpu.make_async_copy(dqo.at[rows], dq.at[rows], lsem.at[half])

    def put_out(half):
        rows = slice(half * R * 12, (half + 1) * R * 12)
        dqo[rows] = tmp[rows].astype(BF)
        out_copy(half).start()

    core_send(1)
    for h in range(H):
        for i in range(W // 128 + 2):
            qs[h, i // 2, i % 2 * 128 : i % 2 * 128 + 128, :] = kv[h, 0, i * 128 : i * 128 + 128, :].T
    query_gradients(0, 0, 2, qs, dss, tmp)
    red1(1)
    query_gradients(0, 2, 6, qs, dss, tmp)
    put_out(0)
    red2(1)
    query_gradients(1, 0, 3, qs, dss, tmp)
    red3(1)
    query_gradients(1, 3, 6, qs, dss, tmp)
    put_out(1)
    red4(1)
    for half in range(2):
        out_copy(half).wait()
    for h in range(H):
        for kind in range(2):
            r = routes(h, kind)
            for n in range(10):
                pl.when(r[n][0])(lambda n=n, r=r: r[n][1]().wait_send())
            for j in range(4):
                pl.when(me >= 2 * j + 1)(lambda h=h, kind=kind, j=j: core_copy(h, kind, j).wait_send())
            for j in range(2):
                pl.when(me >= 2 + 4 * j)(lambda h=h, kind=kind, j=j: y_copy(h, kind, j).wait_send())
                pl.when(x >= 2 - j)(lambda h=h, kind=kind, j=j: x_copy(h, kind, j).wait_send())


def fused(q2, do2, k2, v2, bs):
    vm = pl.BlockSpec(memory_space=pltpu.VMEM)
    hbm = pl.BlockSpec(memory_space=pl.ANY)
    tile = pltpu.VMEM((KW // 8, 8, 256), F32)
    stats = pltpu.VMEM((len(chunks()) + 1, 8, 256), F32)
    dma = pltpu.SemaphoreType.DMA
    return pl.pallas_call(
        kernel,
        out_shape=(jax.ShapeDtypeStruct((R * 24, D), BF), jax.ShapeDtypeStruct((R * 2, D), F32),
                   jax.ShapeDtypeStruct((R * 2, D), F32)),
        in_specs=[hbm] * 5,
        out_specs=(hbm, vm, vm),
        scratch_shapes=[
            pltpu.VMEM((R * 24, D), BF), pltpu.VMEM((24, KP, 256), BF),
            pltpu.VMEM((H, G, R, D), BF), pltpu.VMEM((H, G, R, D), BF),
            pltpu.VMEM((R * 24, D), F32), pltpu.VMEM((4, KW, 128), F32),
            pltpu.VMEM((2, R * H, D), BF), pltpu.VMEM((1, R), jnp.int32),
            pltpu.VMEM((H, 2, W + R, D), BF), pltpu.VMEM((H, 2, W + R, D), F32),
            tile, tile, stats, tile, tile, stats,
            pltpu.VMEM((H, 2, 4, R, D), BF), pltpu.VMEM((H, 2, 4, R, D), BF),
            pltpu.VMEM((H, 2, 2, R, D), BF), pltpu.VMEM((H, 2, 2, R, D), BF),
            pltpu.VMEM((H, 2, 2, R, D), BF), pltpu.VMEM((H, 2, 2, R, D), BF),
            dma((5,)), dma((H, 2, 10)), dma((H, 2, 9)),
            dma((H, 2, 4)), dma((H, 2, 4)), dma((H, 2, 2)), dma((H, 2, 2)), dma((H, 2, 2)), dma((H, 2, 2)),
        ],
        compiler_params=pltpu.CompilerParams(collective_id=0, has_side_effects=True, vmem_limit_bytes=VLIM),
    )(q2, do2, k2, v2, bs)


def finish_kernel(dq, gk, gv, dq_out, gk_out, gv_out, narrow, wide, kin, sin, sout):
    n = 4
    rows = R * 24 // n
    ins = [pltpu.make_async_copy(dq.at[pl.ds(i * rows, rows)], narrow.at[i], sin.at[i]) for i in range(n)]
    ins += [pltpu.make_async_copy(src, kin.at[i], sin.at[n + i]) for i, src in enumerate((gk, gv))]
    outs = [pltpu.make_async_copy(wide.at[i], dq_out.at[pl.ds(i * rows, rows)], sout.at[i]) for i in range(n)]
    outs += [pltpu.make_async_copy(kin.at[2], gk_out, sout.at[n]), pltpu.make_async_copy(kin.at[1], gv_out, sout.at[n + 1])]
    for a in ins:
        a.start()
    for i in range(n):
        ins[i].wait()
        wide[i] = narrow[i].astype(F32) * SC
        outs[i].start()
    ins[n].wait()
    kin[2] = kin[0] * SC
    outs[n].start()
    ins[n + 1].wait()
    outs[n + 1].start()
    for a in outs:
        a.wait()


def finish(dq, gk, gv):
    n = 4
    hbm = pl.BlockSpec(memory_space=pl.ANY)
    return pl.pallas_call(
        finish_kernel,
        out_shape=[jax.ShapeDtypeStruct(a.shape, F32) for a in (dq, gk, gv)],
        in_specs=[hbm] * 3,
        out_specs=[hbm] * 3,
        scratch_shapes=[
            pltpu.VMEM((n, R * 24 // n, D), BF), pltpu.VMEM((n, R * 24 // n, D), F32), pltpu.VMEM((3, R * 2, D), F32),
            pltpu.SemaphoreType.DMA((n + 2,)), pltpu.SemaphoreType.DMA((n + 2,)),
        ],
        compiler_params=pltpu.CompilerParams(vmem_limit_bytes=62 * 2**20),
    )(dq, gk, gv)


def shards(queries, keys, values, output_gradient, band_start):
    q2 = queries.transpose(0, 2, 1, 3).reshape(R * 24, D)
    d2 = output_gradient.transpose(0, 2, 1, 3).reshape(R * 24, D)
    dq, gk, gv = fused(q2, d2, keys.reshape(R * H, D), values.reshape(R * H, D), band_start.reshape(1, R))
    dq, gk, gv = finish(dq, gk, gv)
    return dq.reshape(R, G, H, D).transpose(0, 2, 1, 3), gk.reshape(R, H, D), gv.reshape(R, H, D)


def solution(mesh):
    rows = P(("rep", "ctx"), "kv", None, None)
    keyed = P(("rep", "ctx"), "kv", None)
    return jax.shard_map(shards, mesh=mesh, in_specs=(rows, keyed, keyed, rows, P(("rep", "ctx"))),
                         out_specs=(rows, keyed, keyed), check_vma=False)
```

```python
import functools, math
import jax, jax.numpy as jnp
from jax import lax
from jax.experimental import pallas as pl
from jax.experimental.pallas import tpu as pltpu
from jax.sharding import PartitionSpec as P

R = 256
G = 12
H = 2
D = 128
W = 2048
CH = 128
SZ = 352
QT = 64
KW = W + QT
KP = W + 128
NB = W // R
SC = D**-0.5
C2 = SC * math.log2(math.e)
NEG = -1e30
VLIM = 63 * 2**20
NT = (((1,), (1,)), ((), ()))
NN = (((1,), (0,)), ((), ()))
TN = (((0,), (0,)), ((), ()))
MESH = pl.DeviceIdType.MESH
BF = jnp.bfloat16
F32 = jnp.float32


def dot(a, b, dims):
    return lax.dot_general(a, b, dims, preferred_element_type=F32)


def chunks():
    return [(o, min(SZ, KW - o)) for o in range(0, KW, SZ)]


def unit_rows(ref, h, gq, qt):
    return ref[h, pl.ds(gq * 4, 4), pl.ds(pl.multiple_of(qt * QT, QT), QT), :].reshape(256, D)


def unit_keys(qt, o, n):
    return pl.ds(pl.multiple_of(qt * QT + o, 16), n)


def stage_a(h, gq, qt, qs, dos, kv, bias, p, dp, st, backwards=False):
    qu = unit_rows(qs, h, gq, qt)
    du = unit_rows(dos, h, gq, qt)
    m = jnp.full((1, 8, 256), NEG, F32)
    l = jnp.zeros((1, 8, 256), F32)
    dd = l
    numbered = list(enumerate(chunks()))
    for i, (o, n) in numbered[::-1] if backwards else numbered:
        keys = unit_keys(qt, o, n)
        s = dot(kv[h, 0, keys, :], qu, NT) * C2
        g = dot(kv[h, 1, keys, :], du, NT)
        b = bias[qt, o : o + n, :]
        s = (s + jnp.concatenate([b, b], 1)).reshape(n // 8, 8, 256)
        g = g.reshape(n // 8, 8, 256)
        mn = jnp.maximum(m, jnp.max(s, 0, keepdims=True))
        al = jnp.exp2(m - mn)
        e = jnp.exp2(s - mn)
        l = l * al + jnp.sum(e, 0, keepdims=True)
        dd = dd * al + jnp.sum(e * g, 0, keepdims=True)
        p[o // 8 : (o + n) // 8] = e
        dp[o // 8 : (o + n) // 8] = g
        st[i] = mn[0]
        m = mn
        yield 1
    mm = jnp.max(m, 1, keepdims=True)
    e = jnp.exp2(m - mm)
    il = 1.0 / jnp.sum(l * e, 1, keepdims=True)
    ds = jnp.sum(dd * e, 1, keepdims=True) * il
    nc = len(chunks())
    for i in range(nc):
        st[i] = jnp.exp2(st[i] - mm[0]) * il[0]
    st[nc] = jnp.broadcast_to(ds[0], (8, 256))
    yield 1


def stage_b(h, gq, qt, u, pad, qs, dos, p, dp, st, dkv, dss):
    qu = unit_rows(qs, h, gq, qt)
    du = unit_rows(dos, h, gq, qt)
    dsum = st[len(chunks())][None]
    for i, (o, n) in enumerate(chunks()):
        keys = unit_keys(qt, o, n)
        w = p[o // 8 : (o + n) // 8] * st[i][None]
        x = w * (dp[o // 8 : (o + n) // 8] - dsum)
        wb = w.reshape(n, 256).astype(BF)
        xb = x.reshape(n, 256).astype(BF)
        dkv[h, 1, keys, :] += dot(wb, du, NN)
        dkv[h, 0, keys, :] += dot(xb, qu, NN)
        dss[u, pad + o : pad + o + n, :] = xb
        yield 1


def query_gradients(half, first, last, kt, dss, dq):
    def body(i, _):
        h = i // 3
        gq = i % 3
        u = (h * 6 + gq * 2 + half) * 2
        tiles = [kt[h, i // 2, i % 2 * 128 : i % 2 * 128 + 128, :] for i in range(half, half + KP // 128)]
        keys = jnp.concatenate(tiles, 1)
        for side in range(2):
            t = dot(keys, dss[u + side], NN).T
            for k in range(4):
                row = (half * 2 + side) * QT * 24 + (gq * 4 + k) * 2 + h
                dq[pl.ds(row, QT, stride=24), :] = t[k * QT : (k + 1) * QT]
        return 0

    lax.fori_loop(first, last, body, 0)


def together(*steps):
    steps = list(steps)
    while steps:
        for s in list(steps):
            if next(s, 0) == 0:
                steps.remove(s)


def kernel(q2, do2, k2, v2, bs, dq, gk, gv, dqo, dss, qs, dos, tmp, bias, kvin, first, kv, dkv, p0, dp0, st0, p1, dp1, st1,
           cs, cr, ys, yr, xs, xr, lsem, gs, gr, css, crs, yss, yrs, xss, xrs):
    me = lax.axis_index("ctx")
    x = me // 4
    yl = (me // 2) % 2
    c = me % 2
    base = me * R
    core = me + 1 - 2 * c
    ypar = me + 2 - 4 * yl

    own = [
        pltpu.make_async_copy(k2, kvin.at[0], lsem.at[2]),
        pltpu.make_async_copy(v2, kvin.at[1], lsem.at[3]),
        pltpu.make_async_copy(bs, first, lsem.at[4]),
    ]
    for a in own:
        a.start()
    loads = [pltpu.make_async_copy(q2, dqo, lsem.at[0]), pltpu.make_async_copy(do2, dqo, lsem.at[1])]
    loads[0].start()

    barrier = pltpu.get_barrier_semaphore()
    for t in (core, ypar):
        pl.semaphore_signal(barrier, inc=1, device_id={"ctx": t}, device_id_type=MESH)

    for there, t in ((x < 3, me + 4), (x > 0, me - 4), (x < 2, me + 8), (x > 1, me - 8)):

        @pl.when(there)
        def _():
            pl.semaphore_signal(barrier, inc=1, device_id={"ctx": t}, device_id_type=MESH)

    for kind in range(2):
        own[kind].wait()
        tmp[kind * 2 * R : (kind + 1) * 2 * R] = kvin[kind].astype(F32)
        for h in range(H):
            kv[h, kind, NB * R :] = tmp[pl.ds(kind * 2 * R + h, R, stride=2), :].astype(BF)

    pl.semaphore_wait(barrier, 4 + jnp.where((x == 1) | (x == 2), 1, 0))

    def rc(src, dst, ss, rs, to):
        return pltpu.make_async_remote_copy(src_ref=src, dst_ref=dst, send_sem=ss, recv_sem=rs,
                                            device_id={"ctx": to}, device_id_type=MESH)

    def block(h, kind, slot):
        return kv.at[h, kind, pl.ds(slot * R, R)]

    def part(slot):
        return pl.ds(slot * R, R)

    def routes(h, kind):
        def one(num, src_slot, slot, to):
            return rc(block(h, kind, src_slot), block(h, kind, slot), gs.at[h, kind, num], gr.at[h, kind, slot], to)

        return {
            0: (x < 3, lambda: one(0, 8, 4, me + 4)),
            1: (yl == 0, lambda: one(1, 8, 6, ypar)),
            2: (c == 0, lambda: one(2, 8, 7, core)),
            3: (x < 2, lambda: one(3, 8, 0, me + 8)),
            4: (x > 0, lambda: one(4, 4, 2 + 4 * yl, ypar)),
            5: (x > 0, lambda: one(5, 4, 3 + 2 * c, core)),
            6: (me >= 2, lambda: one(6, 6, 5 + 2 * c, core)),
            7: ((x > 1) & (yl == 1), lambda: one(7, 0, 2, ypar)),
            8: ((x > 1) & (c == 1), lambda: one(8, 0, 1, core)),
            9: (me >= 6, lambda: one(9, 2, 1 + 2 * c, core)),
        }

    def go(h, nums):
        for kind in range(2):
            r = routes(h, kind)
            for n in nums:
                pl.when(r[n][0])(lambda n=n, r=r: r[n][1]().start())

    def arrived(h, kind, slot):
        @pl.when(me >= 8 - slot)
        def _():
            rc(block(h, kind, slot), block(h, kind, slot), gs.at[h, kind, 0], gr.at[h, kind, slot], core).wait_recv()

    def after(h, slot, nums):
        for kind in range(2):
            arrived(h, kind, slot)
            r = routes(h, kind)
            for n in nums:
                pl.when(r[n][0])(lambda n=n, r=r: r[n][1]().start())

    def odd_slots(h):
        for kind in range(2):
            for slot in (7, 5, 3, 1):
                arrived(h, kind, slot)

    def core_copy(h, kind, j):
        return rc(cs.at[h, kind, j], cr.at[h, kind, j], css.at[h, kind, j], crs.at[h, kind, j], core)

    def y_copy(h, kind, j):
        return rc(ys.at[h, kind, j], yr.at[h, kind, j], yss.at[h, kind, j], yrs.at[h, kind, j], ypar)

    def x_copy(h, kind, j):
        return rc(xs.at[h, kind, j], xr.at[h, kind, j], xss.at[h, kind, j], xrs.at[h, kind, j], me - 8 + 4 * j)

    def core_send(h):
        for j in (3, 2, 0, 1):
            @pl.when(me >= 2 * j + 1)
            def _():
                for kind in (1, 0):
                    cs[h, kind, j] = dkv[h, kind, part(7 - 2 * j), :].astype(BF)
                    core_copy(h, kind, j).start()

    def core_add(h, kind, j):
        @pl.when(core >= 2 * j + 1)
        def _():
            core_copy(h, kind, j).wait_recv()
            to = 8 - 2 * j - 2 * c
            dkv[h, kind, part(to), :] += cr[h, kind, j].astype(F32)

    def y_send(h, kind, j):
        @pl.when(me >= 2 + 4 * j)
        def _():
            ys[h, kind, j] = dkv[h, kind, part(6 - 4 * j), :].astype(BF)
            y_copy(h, kind, j).start()

    def y_add(h, kind, j):
        @pl.when(ypar >= 2 + 4 * j)
        def _():
            y_copy(h, kind, j).wait_recv()
            to = 8 - 4 * (j + yl)
            dkv[h, kind, part(to), :] += yr[h, kind, j].astype(F32)

    def x_send(h, kind, j):
        @pl.when(x >= 2 - j)
        def _():
            xs[h, kind, j] = dkv[h, kind, part(4 * j), :].astype(BF)
            x_copy(h, kind, j).start()

    def x_add(h, kind, j):
        @pl.when(x <= 1 + j)
        def _():
            x_copy(h, kind, j).wait_recv()
            dkv[h, kind, part(8), :] += xr[h, kind, j].astype(F32)

    def red1(h):
        for kind in (1, 0):
            core_add(h, kind, 3)
            core_add(h, kind, 2)
            y_send(h, kind, 1)
            pl.when(yl == 0)(lambda: x_send(h, kind, 0))
        for kind in (1, 0):
            core_add(h, kind, 0)
            core_add(h, kind, 1)
            y_send(h, kind, 0)

    def red2(h):
        for kind in (1, 0):
            y_add(h, kind, 1)
            pl.when(yl == 0)(lambda: x_send(h, kind, 1))
            pl.when(yl == 1)(lambda: x_send(h, kind, 0))

    def red3(h):
        for kind in (1, 0):
            y_add(h, kind, 0)
            pl.when(yl == 1)(lambda: x_send(h, kind, 1))

    def red4(h):
        for kind in (1, 0):
            x_add(h, kind, 0)
            x_add(h, kind, 1)
            t = dkv[h, kind, part(8), :]
            (gk, gv)[kind][pl.ds(h, R, stride=2), :] = t

    go(0, (0, 1, 2))
    go(0, (3,))

    for slot in range(8):
        @pl.when(me < 8 - slot)
        def _():
            for h in range(H):
                for kind in range(2):
                    kv[h, kind, part(slot), :] = jnp.zeros((R, D), BF)
    row = base + lax.broadcasted_iota(jnp.int32, (1, R), 1)
    own[2].wait()
    start = first[...]
    for qt in range(4):
        sl = slice(qt * QT, qt * QT + QT)
        low = jnp.concatenate([start[:, sl]] * 2, 1)
        high = jnp.concatenate([row[:, sl]] * 2, 1)

        def body(i, _):
            key = base - W + qt * QT + i * QT + lax.broadcasted_iota(jnp.int32, (QT, 128), 0)
            ok = (key >= low) & (key <= high)
            bias[qt, pl.ds(pl.multiple_of(i * QT, QT), QT), :] = jnp.where(ok, 0.0, NEG)
            return 0

        lax.fori_loop(0, KW // QT, body, 0)
    for u in range(0, 24, 2):
        dss[u, KW:, :] = jnp.zeros((QT, 256), BF)
        dss[u + 1, :QT, :] = jnp.zeros((QT, 256), BF)

    def unpack(n, src, dst):
        loads[n].wait()
        tmp[...] = src[...].astype(F32)
        if n == 0:
            loads[1].start()

        def body(g, _):
            for h in range(H):
                dst[h, g] = tmp[pl.ds(g * 2 + h, R, stride=24), :].astype(BF)
            return 0

        lax.fori_loop(0, G, body, 0)

    unpack(0, dqo, qs)
    after(0, 4, (4, 5))
    unpack(1, dqo, dos)
    dkv[...] = jnp.zeros_like(dkv)
    after(0, 6, (6,))
    opening = stage_a(0, 0, 0, qs, dos, kv, bias, p0, dp0, st0, backwards=True)
    for slot, nums, odd in ((6, None, 7), (0, (7, 8), 5), (2, (9,), 3), (None, None, 1)):
        if nums:
            after(0, slot, nums)
        for kind in range(2):
            arrived(0, kind, odd)
        next(opening)
    together(opening)

    steps = {
        0: lambda: go(1, (0, 1, 2, 3)),
        1: lambda: after(1, 4, (4, 5)),
        2: lambda: after(1, 6, (6,)),
        3: lambda: after(1, 0, (7, 8)),
        4: lambda: after(1, 2, (9,)),
        5: lambda: odd_slots(1),
        6: lambda: core_send(0),
        7: lambda: red1(0),
        9: lambda: red2(0),
        10: lambda: red3(0),
        11: lambda: red4(0),
    }

    def unit(it, _):
        for k, f in steps.items():
            if k < 11:
                pl.when(it == k)(f)
        def place(i):
            return i // 6, i % 6 // 2, i % 2 * 2

        h, gq, qt = place(it)
        h2, gq2, qt2 = place(it + 1)
        together(
            stage_a(h, gq, qt + 1, qs, dos, kv, bias, p1, dp1, st1),
            stage_b(h, gq, qt, it * 2, 0, qs, dos, p0, dp0, st0, dkv, dss),
        )
        together(
            stage_a(h2, gq2, qt2, qs, dos, kv, bias, p0, dp0, st0),
            stage_b(h, gq, qt + 1, it * 2 + 1, QT, qs, dos, p1, dp1, st1, dkv, dss),
        )
        return 0

    lax.fori_loop(0, 11, unit, 0)
    steps[11]()
    together(
        stage_a(1, 2, 3, qs, dos, kv, bias, p1, dp1, st1),
        stage_b(1, 2, 2, 22, 0, qs, dos, p0, dp0, st0, dkv, dss),
    )
    together(stage_b(1, 2, 3, 23, QT, qs, dos, p1, dp1, st1, dkv, dss))
    def out_copy(half):
        rows = pl.ds(half * R * 12, R * 12)
        return pltpu.make_async_copy(dqo.at[rows], dq.at[rows], lsem.at[half])

    def put_out(half):
        rows = slice(half * R * 12, (half + 1) * R * 12)
        dqo[rows] = tmp[rows].astype(BF)
        out_copy(half).start()

    core_send(1)
    for h in range(H):
        for i in range(W // 128 + 2):
            qs[h, i // 2, i % 2 * 128 : i % 2 * 128 + 128, :] = kv[h, 0, i * 128 : i * 128 + 128, :].T
    query_gradients(0, 0, 2, qs, dss, tmp)
    red1(1)
    query_gradients(0, 2, 6, qs, dss, tmp)
    put_out(0)
    red2(1)
    query_gradients(1, 0, 3, qs, dss, tmp)
    red3(1)
    query_gradients(1, 3, 6, qs, dss, tmp)
    put_out(1)
    red4(1)
    for half in range(2):
        out_copy(half).wait()
    for h in range(H):
        for kind in range(2):
            r = routes(h, kind)
            for n in range(10):
                pl.when(r[n][0])(lambda n=n, r=r: r[n][1]().wait_send())
            for j in range(4):
                pl.when(me >= 2 * j + 1)(lambda h=h, kind=kind, j=j: core_copy(h, kind, j).wait_send())
            for j in range(2):
                pl.when(me >= 2 + 4 * j)(lambda h=h, kind=kind, j=j: y_copy(h, kind, j).wait_send())
                pl.when(x >= 2 - j)(lambda h=h, kind=kind, j=j: x_copy(h, kind, j).wait_send())


def fused(q2, do2, k2, v2, bs):
    vm = pl.BlockSpec(memory_space=pltpu.VMEM)
    hbm = pl.BlockSpec(memory_space=pl.ANY)
    tile = pltpu.VMEM((KW // 8, 8, 256), F32)
    stats = pltpu.VMEM((len(chunks()) + 1, 8, 256), F32)
    dma = pltpu.SemaphoreType.DMA
    return pl.pallas_call(
        kernel,
        out_shape=(jax.ShapeDtypeStruct((R * 24, D), BF), jax.ShapeDtypeStruct((R * 2, D), F32),
                   jax.ShapeDtypeStruct((R * 2, D), F32)),
        in_specs=[hbm] * 5,
        out_specs=(hbm, vm, vm),
        scratch_shapes=[
            pltpu.VMEM((R * 24, D), BF), pltpu.VMEM((24, KP, 256), BF),
            pltpu.VMEM((H, G, R, D), BF), pltpu.VMEM((H, G, R, D), BF),
            pltpu.VMEM((R * 24, D), F32), pltpu.VMEM((4, KW, 128), F32),
            pltpu.VMEM((2, R * H, D), BF), pltpu.VMEM((1, R), jnp.int32),
            pltpu.VMEM((H, 2, W + R, D), BF), pltpu.VMEM((H, 2, W + R, D), F32),
            tile, tile, stats, tile, tile, stats,
            pltpu.VMEM((H, 2, 4, R, D), BF), pltpu.VMEM((H, 2, 4, R, D), BF),
            pltpu.VMEM((H, 2, 2, R, D), BF), pltpu.VMEM((H, 2, 2, R, D), BF),
            pltpu.VMEM((H, 2, 2, R, D), BF), pltpu.VMEM((H, 2, 2, R, D), BF),
            dma((5,)), dma((H, 2, 10)), dma((H, 2, 9)),
            dma((H, 2, 4)), dma((H, 2, 4)), dma((H, 2, 2)), dma((H, 2, 2)), dma((H, 2, 2)), dma((H, 2, 2)),
        ],
        compiler_params=pltpu.CompilerParams(collective_id=0, has_side_effects=True, vmem_limit_bytes=VLIM),
    )(q2, do2, k2, v2, bs)


def finish_kernel(dq, gk, gv, dq_out, gk_out, gv_out, narrow, wide, kin, sin, sout):
    n = 4
    rows = R * 24 // n
    ins = [pltpu.make_async_copy(dq.at[pl.ds(i * rows, rows)], narrow.at[i], sin.at[i]) for i in range(n)]
    ins += [pltpu.make_async_copy(src, kin.at[i], sin.at[n + i]) for i, src in enumerate((gk, gv))]
    outs = [pltpu.make_async_copy(wide.at[i], dq_out.at[pl.ds(i * rows, rows)], sout.at[i]) for i in range(n)]
    outs += [pltpu.make_async_copy(kin.at[2], gk_out, sout.at[n]), pltpu.make_async_copy(kin.at[1], gv_out, sout.at[n + 1])]
    for a in ins:
        a.start()
    for i in range(n):
        ins[i].wait()
        wide[i] = narrow[i].astype(F32) * SC
        outs[i].start()
    ins[n].wait()
    kin[2] = kin[0] * SC
    outs[n].start()
    ins[n + 1].wait()
    outs[n + 1].start()
    for a in outs:
        a.wait()


def finish(dq, gk, gv):
    n = 4
    hbm = pl.BlockSpec(memory_space=pl.ANY)
    return pl.pallas_call(
        finish_kernel,
        out_shape=[jax.ShapeDtypeStruct(a.shape, F32) for a in (dq, gk, gv)],
        in_specs=[hbm] * 3,
        out_specs=[hbm] * 3,
        scratch_shapes=[
            pltpu.VMEM((n, R * 24 // n, D), BF), pltpu.VMEM((n, R * 24 // n, D), F32), pltpu.VMEM((3, R * 2, D), F32),
            pltpu.SemaphoreType.DMA((n + 2,)), pltpu.SemaphoreType.DMA((n + 2,)),
        ],
        compiler_params=pltpu.CompilerParams(vmem_limit_bytes=62 * 2**20),
    )(dq, gk, gv)


def shards(queries, keys, values, output_gradient, band_start):
    q2 = queries.transpose(0, 2, 1, 3).reshape(R * 24, D)
    d2 = output_gradient.transpose(0, 2, 1, 3).reshape(R * 24, D)
    dq, gk, gv = fused(q2, d2, keys.reshape(R * H, D), values.reshape(R * H, D), band_start.reshape(1, R))
    dq, gk, gv = finish(dq, gk, gv)
    return dq.reshape(R, G, H, D).transpose(0, 2, 1, 3), gk.reshape(R, H, D), gv.reshape(R, H, D)


def solution(mesh):
    rows = P(("rep", "ctx"), "kv", None, None)
    keyed = P(("rep", "ctx"), "kv", None)
    return jax.shard_map(shards, mesh=mesh, in_specs=(rows, keyed, keyed, rows, P(("rep", "ctx"))),
                         out_specs=(rows, keyed, keyed), check_vma=False)
```
